256 devices in a mesh: sx: 4 (over x_hi, core), sy: 32 (over y, z), ta: 2 (over x_lo).
Axes of the slice: x: 4 (x_hi: 2, x_lo: 2; x = x_hi * 2 + x_lo), y: 4, z: 8, core: 2. Of those that a mesh axis runs over, the one named last changes fastest.
Arguments:
- forcing: float32 [64, 128, 4096], P('ta', 'sx', 'sy'), may hold values from -12 to 12
- react: float32 [128, 4096], P('sx', 'sy'), may hold values from 0.05 to 1
- initial: float32 [128, 4096], P('sx', 'sy'), may hold values from -8 to 8
Outputs:
- solution: float32 [64, 128, 4096], P('ta', 'sx', 'sy')
- square_means: float32 [3], replicated
The draws below stay inside these ranges and needn't reach their ends.
All inputs are finite; a program needn't handle non-finite values.
Results may differ from the reference program's by a relative error of at most 0.0001.
Values sent between devices are 32-bit elements; how exact they have to be, the bound alone decides.
A program may use at most 64 MiB of HBM per device.

```python
import math
import jax
import jax.numpy as jnp
from jax import lax

L = 64
SWEEPS = 8
ITERS = 2
NX = 128
NY = 4096


def draw_forcing(key, part):
    across = jnp.arange(NX, dtype=jnp.float32) / NX
    along = jnp.arange(NY, dtype=jnp.float32) / NY
    amplitude = 1.0 + across[:, None] + along[None, :]
    values = jnp.clip(jax.random.normal(key, (L, NX, NY), jnp.float32), -4.0, 4.0)
    return values * amplitude[None]


def block_levels(stream_key, shape, cuts, least, largest):
    def one(axis_at, shards_of):
        heights = jax.random.uniform(jax.random.fold_in(jax.random.fold_in(stream_key, 6), axis_at), (shards_of,), jnp.float32, least / len(cuts), largest / len(cuts))
        return jnp.repeat(jnp.exp(heights), shape[axis_at] // shards_of).reshape((-1,) + (1,) * (len(shape) - axis_at - 1))

    gain = one(*cuts[0])
    for cut in cuts[1:]:
        gain = gain * one(*cut)
    return gain


def scatter_about(key, shape, deviation, reach, cuts=(), kind=jnp.bfloat16):
    factor_of = block_levels(key, shape, cuts, -0.22, 0.18) if cuts else 1.0
    entries = jax.random.normal(key, shape, jnp.float32) * deviation * factor_of
    return jnp.minimum(jnp.maximum(entries, -reach), reach).astype(kind)


def setup_inputs(seed: int = 0) -> dict:
    arg_keys = jax.random.split(jax.random.key(seed), 4)
    forcing = draw_forcing(jax.random.fold_in(arg_keys[3], 71), 0)
    react = jnp.clip(jnp.exp(math.log(1.0) - 2.9957323 * jax.random.uniform(arg_keys[1], (NX, NY), jnp.float32) ** block_levels(arg_keys[1], (NX, NY), ((0, 4), (1, 32)), -0.2, 0.2)), 0.05, 1.0)
    initial = scatter_about(arg_keys[2], (NX, NY), 2.0, 8.0, ((0, 4), (1, 32)), jnp.float32)
    return dict(forcing=forcing, react=react, initial=initial)


ALPHA = 0.1
STEP = 2.0


def neighbours(padded):
    return padded[..., 2:, 1:-1] + padded[..., :-2, 1:-1] + padded[..., 1:-1, 2:] + padded[..., 1:-1, :-2]


def apply_operator(field, react):
    widths = [(0, 0)] * (field.ndim - 2) + [(1, 1), (1, 1)]
    return (4.0 + react) * field - neighbours(jnp.pad(field, widths))


def residual_of(solution, forcing, react, initial):
    earlier = jnp.concatenate([initial[None], solution[:-1]], 0)
    return forcing - (solution - earlier) / STEP - apply_operator(solution, react)


def angle_table(left_index, right_index, length):
    phase = (left_index[:, None] * right_index[None, :]) % length
    return 2.0 * math.pi * phase.astype(jnp.float32) / length


def complex_product(inverse_re, inverse_im, value_re, value_im):
    return inverse_re * value_re - inverse_im * value_im, inverse_re * value_im + inverse_im * value_re


def precondition(residual, react):
    decay_rate = ALPHA ** (1.0 / L)
    time_index = jnp.arange(L, dtype=jnp.int32)
    exponent = time_index.astype(jnp.float32)
    scaled = residual * (decay_rate ** exponent)[:, None, None]
    angles = angle_table(time_index, time_index, L)
    cosine_table = jnp.cos(angles)
    sine_table = jnp.sin(angles)
    flattened = scaled.reshape(L, -1)
    spec_re = jnp.dot(cosine_table, flattened, precision=lax.Precision.HIGHEST).reshape(residual.shape)
    spec_im = jnp.dot(-sine_table, flattened, precision=lax.Precision.HIGHEST).reshape(residual.shape)
    phases = 2.0 * math.pi * exponent / L
    shift_re = (1.0 - decay_rate * jnp.cos(phases)) / STEP
    shift_im = decay_rate * jnp.sin(phases) / STEP

    def sweep_one(pieces):
        rhs_re, rhs_im, one_re, one_im = pieces
        diag_re = one_re + 4.0 + react
        diag_im = one_im
        magnitude = diag_re * diag_re + diag_im * diag_im
        inverse_re = diag_re / magnitude
        inverse_im = -diag_im / magnitude
        iterate_re, iterate_im = complex_product(inverse_re, inverse_im, rhs_re, rhs_im)
        for sweep_index in range(SWEEPS - 1):
            summed_re = rhs_re + neighbours(jnp.pad(iterate_re, 1))
            summed_im = rhs_im + neighbours(jnp.pad(iterate_im, 1))
            iterate_re, iterate_im = complex_product(inverse_re, inverse_im, summed_re, summed_im)
        return iterate_re, iterate_im

    iterate_re, iterate_im = lax.map(sweep_one, (spec_re, spec_im, shift_re, shift_im))
    recovered = (jnp.dot(cosine_table, iterate_re.reshape(L, -1), precision=lax.Precision.HIGHEST)
                 - jnp.dot(sine_table, iterate_im.reshape(L, -1), precision=lax.Precision.HIGHEST)) / L
    return recovered.reshape(residual.shape) * (decay_rate ** (-exponent))[:, None, None]


def reference(forcing, react, initial):
    solution = jnp.zeros_like(forcing)
    cell_count = forcing.shape[0] * forcing.shape[1] * forcing.shape[2]
    square_list = []
    for iteration in range(ITERS):
        residual = residual_of(solution, forcing, react, initial)
        square_list.append(jnp.sum(residual * residual) / cell_count)
        solution = solution + precondition(residual, react)
    residual = residual_of(solution, forcing, react, initial)
    square_list.append(jnp.sum(residual * residual) / cell_count)
    return solution, jnp.stack(square_list)
```

```python
import functools

import jax
import jax.numpy as jnp
from jax import lax
from jax.experimental import pallas as pl
from jax.experimental.pallas import tpu as pltpu
from jax.sharding import PartitionSpec as P

SWEEPS = 8
ALPHA = 0.1
STEP = 2.0
CORNER = ALPHA / STEP
OWN = 16
HALO = 16
WIDE = OWN + 2 * HALO
LINE = 8
MESH = pl.DeviceIdType.MESH


def iota(axis):
    return lax.broadcasted_iota(jnp.int32, (8, 128), axis)


def place_of(p):
    return 2 * (p // 4) + p % 2, (p // 2) % 2


def swap_groups(v):
    lane = iota(1)
    low = lane < 64
    even = (lane // 32) % 2 == 0
    a = [
        jnp.where(low, v[0], pltpu.roll(v[2], 64, 1)),
        jnp.where(low, v[1], pltpu.roll(v[3], 64, 1)),
        jnp.where(low, pltpu.roll(v[0], 64, 1), v[2]),
        jnp.where(low, pltpu.roll(v[1], 64, 1), v[3]),
    ]
    return [
        jnp.where(even, a[0], pltpu.roll(a[1], 32, 1)),
        jnp.where(even, pltpu.roll(a[0], 96, 1), a[1]),
        jnp.where(even, a[2], pltpu.roll(a[3], 32, 1)),
        jnp.where(even, pltpu.roll(a[2], 96, 1), a[3]),
    ]


def kernel(ny, nz, f, react, init, out, stat, S, rcv, tmp, rsend, rrecv, rext, Rx, CR, U, CF, E,
           M, O, redx, redy, redz, a_s, a_r, c_s, c_r, h_s, h_r, o_s, o_r, x_s, x_r, y_s, y_r,
           z_s, z_r, l_s):
    sx, sy, ta = lax.axis_index("sx"), lax.axis_index("sy"), lax.axis_index("ta")
    nsy = ny * nz
    p = 4 * (sx // 2) + 2 * ta + sx % 2
    odd = sy % 2

    def slice_of(q):
        return q + odd * (7 - 2 * q)

    d = slice_of(p)

    def in_line(q):
        a, b = place_of(q)
        return {"sx": a, "sy": sy, "ta": b}

    def beside(step):
        q = d + step
        inside = jnp.logical_and(q >= 0, q <= 7)
        s = jnp.where(inside, sy, lax.rem(sy + step + nsy, nsy))
        e = jnp.where(inside, slice_of(jnp.clip(q, 0, 7)), p)
        a, b = place_of(e)
        return {"sx": a, "sy": s, "ta": b}

    def in_y(k):
        return {"sx": sx, "sy": lax.rem(sy + nz * k, nsy), "ta": ta}

    def in_z(k):
        z = lax.rem(sy, nz)
        return {"sx": sx, "sy": sy - z + lax.rem(z + k, nz), "ta": ta}

    left, right = beside(-1), beside(1)
    barrier = pltpu.get_barrier_semaphore()
    peers = [in_line(lax.rem(p + k, LINE)) for k in range(1, LINE)]
    peers += [left, right]
    peers += [in_y(k) for k in range(1, ny)]
    peers += [in_z(k) for k in range(1, nz)]
    for peer in peers:
        pl.semaphore_signal(barrier, inc=1, device_id=peer, device_id_type=MESH)

    def remote(src, dst, s_sem, r_sem, peer):
        return pltpu.make_async_remote_copy(
            src_ref=src, dst_ref=dst, send_sem=s_sem, recv_sem=r_sem, device_id=peer,
            device_id_type=MESH,
        )

    tmp[...] = jnp.zeros_like(tmp)
    tmp[pl.ds(pl.multiple_of(sx * 32, 32), 32), :] = react[...]
    rsend[...] = tmp[...].T
    opening = jnp.where(ta == 0, 1.0 / STEP, 0.0)
    for m in range(8):
        b = m % 4
        q = lax.rem(m // 4 + ta, 2)
        planes = [f[8 * b + 2 * g + q] for g in range(4)]
        if m == 0:
            planes[0] = planes[0] + opening * init[...]
        S[pl.ds(m, 128, stride=8), :] = jnp.concatenate(planes, axis=0).T

    pl.semaphore_wait(barrier, len(peers))

    copies_c = []
    for k in range(1, 4):
        to = lax.rem(sx + k, 4)
        q = 4 * (to // 2) + 2 * ta + to % 2
        rows = pl.ds(pl.multiple_of(slice_of(q) * OWN, OWN), OWN)
        c = remote(rsend.at[rows], rrecv.at[sx], c_s.at[k], c_r.at[k],
                   {"sx": to, "sy": sy, "ta": ta})
        c.start()
        copies_c.append(c)
    copies_a = []
    for k in range(1, LINE):
        q = lax.rem(p + k, LINE)
        rows = pl.ds(pl.multiple_of(slice_of(q) * 128, 128), 128)
        c = remote(S.at[rows], rcv.at[p], a_s.at[k], a_r.at[k], in_line(q))
        c.start()
        copies_a.append(c)
    mine = pltpu.make_async_copy(S.at[pl.ds(pl.multiple_of(d * 128, 128), 128)], rcv.at[p],
                                 l_s.at[0])
    mine.start()
    rrecv[sx] = rsend[pl.ds(pl.multiple_of(d * OWN, OWN), OWN), :]
    for c in copies_c:
        c.wait()
    rext[pl.ds(HALO, OWN), :] = (rrecv[0] + rrecv[1]) + (rrecv[2] + rrecv[3])
    halo_c = [
        remote(rext.at[pl.ds(HALO, OWN)], rext.at[pl.ds(HALO + OWN, HALO)], h_s.at[0], h_r.at[0],
               left),
        remote(rext.at[pl.ds(HALO, OWN)], rext.at[pl.ds(0, HALO)], h_s.at[1], h_r.at[1], right),
    ]
    for c in halo_c:
        c.start()

    sub = iota(0)
    lane = iota(1)
    first = sub == 0

    def coefficients(col, inside):
        r = jnp.broadcast_to(rext[pl.ds(col, 1), :], (8, 128))
        c = inside / (1.0 / STEP + 4.0 + r)
        cp = c / STEP
        q2 = cp * cp
        q4 = q2 * q2
        q = q4 * q4
        qq = q * q
        qqqq = qq * qq
        CF[col, 0] = c
        CF[col, 1] = cp
        CF[col, 2] = jnp.where(sub < 1, ALPHA * q, q)
        CF[col, 3] = jnp.where(sub < 2, ALPHA * qq, qq)
        CF[col, 4] = jnp.where(sub < 4, ALPHA * qqqq, qqqq)
        ks = cp / (1.0 - ALPHA * (qqqq * qqqq))
        CF[col, 5] = jnp.where(first, ALPHA * ks, ks)

    def solve(g, col):
        cp = CF[col, 1]
        z = [g[0]]
        for l in range(1, 8):
            z.append(g[l] + cp * z[-1])
        a = z[7]
        a = a + CF[col, 2] * pltpu.roll(a, 1, 0)
        a = a + CF[col, 3] * pltpu.roll(a, 2, 0)
        a = a + CF[col, 4] * pltpu.roll(a, 4, 0)
        s = CF[col, 5] * pltpu.roll(a, 1, 0)
        done = []
        for l in range(8):
            done.append(z[l] + s)
            if l < 7:
                s = s * cp
        return done

    def part(l):
        return pl.ds(8 * l, 8)

    def rows_beside(v):
        return (jnp.where(lane == 0, 0.0, pltpu.roll(v, 1, 1))
                + jnp.where(lane == 127, 0.0, pltpu.roll(v, 127, 1)))

    def first_sweep(col, inside):
        coefficients(col, inside)
        c = CF[col, 0]
        g = []
        for l in range(8):
            v = c * Rx[col, part(l), :]
            CR[col, part(l), :] = v
            g.append(v)
        u = solve(g, col)
        for l in range(8):
            U[0, col, part(l), :] = u[l]

    def spread(lo, hi, fn):
        def step(i, carry):
            fn(lo + i)
            return carry

        lax.fori_loop(0, hi - lo, step, 0)

    mine.wait()
    for c in copies_a:
        c.wait()

    def unpack(col, acc):
        rows = pl.ds(pl.multiple_of(8 * col, 8), 8)
        w = []
        for t in range(2):
            v = [rcv[4 * (s // 2) + 2 * t + s % 2, rows, :] for s in range(4)]
            w.append(swap_groups(v))
        for g in range(4):
            even = jnp.where(sub < 4, w[0][g], w[1][g])
            other = pltpu.roll(jnp.where(sub < 4, w[1][g], w[0][g]), 4, 0)
            Rx[HALO + col, part(2 * g), :] = even
            Rx[HALO + col, part(2 * g + 1), :] = other
            acc = acc + even * even + other * other
        return acc

    acc0 = lax.fori_loop(0, OWN, unpack, jnp.zeros((8, 128), jnp.float32))
    halo_r = [
        remote(Rx.at[pl.ds(HALO, OWN)], Rx.at[pl.ds(HALO + OWN, HALO)], h_s.at[2], h_r.at[2],
               left),
        remote(Rx.at[pl.ds(HALO, OWN)], Rx.at[pl.ds(0, HALO)], h_s.at[3], h_r.at[3], right),
    ]
    for c in halo_r:
        c.start()
    spread(HALO, HALO + OWN, lambda col: first_sweep(col, 1.0))
    for c in halo_c:
        c.wait()
    for c in halo_r:
        c.wait()
    at_start = jnp.logical_and(sy == 0, d == 0)
    at_end = jnp.logical_and(sy == nsy - 1, d == 7)
    in_left = jnp.where(at_start, 0.0, 1.0)
    in_right = jnp.where(at_end, 0.0, 1.0)
    spread(0, HALO, lambda col: first_sweep(col, in_left))
    spread(HALO + OWN, WIDE, lambda col: first_sweep(col, in_right))

    def sweep(j, carry):
        now, later = lax.rem(j, 2), lax.rem(j + 1, 2)

        def one(col):
            c = CF[col, 0]
            g = []
            for l in range(8):
                v = U[now, col, part(l), :]
                n = (U[now, col - 1, part(l), :] + U[now, col + 1, part(l), :]) + rows_beside(v)
                g.append(CR[col, part(l), :] + c * n)
            u = solve(g, col)
            for l in range(8):
                U[later, col, part(l), :] = u[l]

        def step(i, carry):
            one(j + 1 + 2 * i)
            one(j + 2 + 2 * i)
            return carry

        lax.fori_loop(0, WIDE // 2 - 1 - j, step, 0)
        return carry

    def left_over(now, last):
        def step(i, acc):
            col = HALO + i

            def change(k, l):
                return U[now, k, part(l), :] - U[1 - now, k, part(l), :]

            for l in range(8):
                r = change(col - 1, l) + change(col + 1, l) + rows_beside(change(col, l))
                if l == 0:
                    e = CORNER * pltpu.roll(U[now, col, part(7), :], 1, 0)
                    e = jnp.where(first, e, 0.0)
                    r = r + (E[col] - e) if last else r - e
                acc = acc + r * r
            return acc

        return lax.fori_loop(0, OWN, step, jnp.zeros((8, 128), jnp.float32))

    lax.fori_loop(0, SWEEPS - 1, sweep, 0)
    acc1 = left_over((SWEEPS - 1) % 2, False)

    def corner(col):
        e = CORNER * pltpu.roll(U[(SWEEPS - 1) % 2, col, part(7), :], 1, 0)
        e = jnp.where(first, e, 0.0)
        E[col] = e
        CR[col, part(0), :] = CR[col, part(0), :] - CF[col, 0] * e

    spread(SWEEPS - 1, WIDE - SWEEPS + 1, corner)
    lax.fori_loop(SWEEPS - 1, 2 * SWEEPS - 1, sweep, 0)
    acc2 = left_over((2 * SWEEPS - 1) % 2, True)

    def total(v):
        return jnp.sum(v, axis=0, keepdims=True)

    redx[p] = jnp.where(sub == 0, total(acc0), jnp.where(sub == 1, total(acc1), jnp.where(
        sub == 2, total(acc2), 0.0)))
    copies_x = []
    for k in range(1, LINE):
        c = remote(redx.at[p], redx.at[p], x_s.at[k], x_r.at[k], in_line(lax.rem(p + k, LINE)))
        c.start()
        copies_x.append(c)

    ended = (2 * SWEEPS - 1) % 2

    def pack(col, carry):
        rows = pl.ds(pl.multiple_of(8 * col, 8), 8)
        w = [[], []]
        for g in range(4):
            even = U[ended, HALO + col, part(2 * g), :]
            other = pltpu.roll(U[ended, HALO + col, part(2 * g + 1), :], 4, 0)
            w[0].append(jnp.where(sub < 4, even, other))
            w[1].append(jnp.where(sub < 4, other, even))
        for t in range(2):
            v = swap_groups(w[t])
            for s in range(4):
                M[4 * (s // 2) + 2 * t + s % 2, rows, :] = v[s]
        return carry

    lax.fori_loop(0, OWN, pack, 0)
    slot = pl.ds(pl.multiple_of(d * 128, 128), 128)
    copies_o = []
    for k in range(1, LINE):
        q = lax.rem(p + k, LINE)
        c = remote(M.at[q], O.at[slot], o_s.at[k], o_r.at[k], in_line(q))
        c.start()
        copies_o.append(c)
    mine = pltpu.make_async_copy(M.at[p], O.at[slot], l_s.at[1])
    mine.start()

    for c in copies_x:
        c.wait()
    sums = redx[0]
    for k in range(1, LINE):
        sums = sums + redx[k]
    if ny > 1:
        y = sy // nz
        redy[y] = sums
        copies_y = []
        for k in range(1, ny):
            c = remote(redy.at[y], redy.at[y], y_s.at[k], y_r.at[k], in_y(k))
            c.start()
            copies_y.append(c)
        for c in copies_y:
            c.wait()
        sums = redy[0]
        for k in range(1, ny):
            sums = sums + redy[k]
    if nz > 1:
        z = lax.rem(sy, nz)
        redz[z] = sums
        copies_z = []
        for k in range(1, nz):
            c = remote(redz.at[z], redz.at[z], z_s.at[k], z_r.at[k], in_z(k))
            c.start()
            copies_z.append(c)

    mine.wait()
    for c in copies_o:
        c.wait()
    for m in range(8):
        b = m % 4
        q = lax.rem(m // 4 + ta, 2)
        x = O[pl.ds(m, 128, stride=8), :].T
        for g in range(4):
            out[8 * b + 2 * g + q] = x[32 * g:32 * g + 32, :]

    if nz > 1:
        for c in copies_z:
            c.wait()
        sums = redz[0]
        for k in range(1, nz):
            sums = sums + redz[k]
    cells = 64.0 * 128.0 * (128.0 * nsy)
    for i in range(3):
        stat[i] = jnp.sum(sums[i:i + 1, :]) / cells


def solution(mesh):
    nsy = mesh.shape["sy"]
    ny, nz = (4, 8) if nsy == 32 else (2, nsy // 2)

    def step(forcing, react, initial):
        vmem = pl.BlockSpec(memory_space=pltpu.VMEM)
        dma = pltpu.SemaphoreType.DMA
        f32 = jnp.float32
        return pl.pallas_call(
            functools.partial(kernel, ny, nz),
            out_shape=(
                jax.ShapeDtypeStruct((32, 32, 128), f32),
                jax.ShapeDtypeStruct((3,), f32),
            ),
            in_specs=[vmem] * 3,
            out_specs=(vmem, pl.BlockSpec(memory_space=pltpu.SMEM)),
            scratch_shapes=[
                pltpu.VMEM((1024, 128), f32),
                pltpu.VMEM((8, 128, 128), f32),
                pltpu.VMEM((128, 128), f32),
                pltpu.VMEM((128, 128), f32),
                pltpu.VMEM((4, OWN, 128), f32),
                pltpu.VMEM((WIDE, 128), f32),
                pltpu.VMEM((WIDE, 64, 128), f32),
                pltpu.VMEM((WIDE, 64, 128), f32),
                pltpu.VMEM((2, WIDE, 64, 128), f32),
                pltpu.VMEM((WIDE, 6, 8, 128), f32),
                pltpu.VMEM((WIDE, 8, 128), f32),
                pltpu.VMEM((8, 128, 128), f32),
                pltpu.VMEM((1024, 128), f32),
                pltpu.VMEM((LINE, 8, 128), f32),
                pltpu.VMEM((max(ny, 2), 8, 128), f32),
                pltpu.VMEM((max(nz, 2), 8, 128), f32),
                dma((8,)), dma((8,)), dma((4,)), dma((4,)), dma((4,)), dma((4,)),
                dma((8,)), dma((8,)), dma((8,)), dma((8,)), dma((max(ny, 2),)),
                dma((max(ny, 2),)), dma((max(nz, 2),)), dma((max(nz, 2),)), dma((2,)),
            ],
            compiler_params=pltpu.CompilerParams(
                collective_id=0, has_side_effects=True, vmem_limit_bytes=48 << 20
            ),
        )(forcing, react, initial)

    placed = (P("ta", "sx", "sy"), P("sx", "sy"), P("sx", "sy"))
    return jax.shard_map(
        step, mesh=mesh, in_specs=placed, out_specs=(P("ta", "sx", "sy"), P(None)),
        check_vma=False,
    )
```

```python
import functools

import jax
import jax.numpy as jnp
from jax import lax
from jax.experimental import pallas as pl
from jax.experimental.pallas import tpu as pltpu
from jax.sharding import PartitionSpec as P

SWEEPS = 8
ALPHA = 0.1
STEP = 2.0
CORNER = ALPHA / STEP
OWN = 16
HALO = 8
WIDE = OWN + 2 * HALO
ENDS = HALO + OWN
LINE = 8
UNROLL = 8
MESH = pl.DeviceIdType.MESH


def iota(axis):
    return lax.broadcasted_iota(jnp.int32, (8, 128), axis)


def place_of(p):
    return 2 * (p // 4) + p % 2, (p // 2) % 2


def swap_groups(v):
    lane = iota(1)
    low = lane < 64
    even = (lane // 32) % 2 == 0
    a = [
        jnp.where(low, v[0], pltpu.roll(v[2], 64, 1)),
        jnp.where(low, v[1], pltpu.roll(v[3], 64, 1)),
        jnp.where(low, pltpu.roll(v[0], 64, 1), v[2]),
        jnp.where(low, pltpu.roll(v[1], 64, 1), v[3]),
    ]
    return [
        jnp.where(even, a[0], pltpu.roll(a[1], 32, 1)),
        jnp.where(even, pltpu.roll(a[0], 96, 1), a[1]),
        jnp.where(even, a[2], pltpu.roll(a[3], 32, 1)),
        jnp.where(even, pltpu.roll(a[2], 96, 1), a[3]),
    ]


def part(l):
    return pl.ds(8 * l, 8)


def kernel(ny, nz, f_hbm, react_hbm, init_hbm, out, stat, f, react, init, S, rcv, tmp, rsend, rrecv,
           rext, Rx, CR, U0, U1, V0, NB, CL, PW, KS, E, M, O, redx, redy, redz, a_s, a_r, c_s, c_r,
           h_s, h_r, o_s, o_r, x_s, x_r, y_s, y_r, z_s, z_r, l_s):
    sx, sy, ta = lax.axis_index("sx"), lax.axis_index("sy"), lax.axis_index("ta")
    nsy = ny * nz
    p = 4 * (sx // 2) + 2 * ta + sx % 2
    odd = sy % 2

    def slice_of(q):
        return q + odd * (7 - 2 * q)

    d = slice_of(p)

    def in_line(q):
        a, b = place_of(q)
        return {"sx": a, "sy": sy, "ta": b}

    def beside(step):
        q = d + step
        inside = jnp.logical_and(q >= 0, q <= 7)
        s = jnp.where(inside, sy, lax.rem(sy + step + nsy, nsy))
        e = jnp.where(inside, slice_of(jnp.clip(q, 0, 7)), p)
        a, b = place_of(e)
        return {"sx": a, "sy": s, "ta": b}

    def in_y(k):
        return {"sx": sx, "sy": lax.rem(sy + nz * k, nsy), "ta": ta}

    def in_z(k):
        z = lax.rem(sy, nz)
        return {"sx": sx, "sy": sy - z + lax.rem(z + k, nz), "ta": ta}

    left, right = beside(-1), beside(1)
    inputs = [
        pltpu.make_async_copy(react_hbm, react, l_s.at[2]),
        pltpu.make_async_copy(init_hbm, init, l_s.at[3]),
        pltpu.make_async_copy(f_hbm, f, l_s.at[4]),
    ]
    for c in inputs:
        c.start()
    barrier = pltpu.get_barrier_semaphore()
    peers = [in_line(lax.rem(p + k, LINE)) for k in range(1, LINE)]
    peers += [left, right]
    peers += [in_y(k) for k in range(1, ny)]
    peers += [in_z(k) for k in range(1, nz)]
    for peer in peers:
        pl.semaphore_signal(barrier, inc=1, device_id=peer, device_id_type=MESH)

    def remote(src, dst, s_sem, r_sem, peer):
        return pltpu.make_async_remote_copy(
            src_ref=src, dst_ref=dst, send_sem=s_sem, recv_sem=r_sem, device_id=peer,
            device_id_type=MESH,
        )

    tmp[...] = jnp.zeros_like(tmp)
    inputs[0].wait()
    tmp[pl.ds(pl.multiple_of(sx * 32, 32), 32), :] = react[...]
    rsend[...] = tmp[...].T
    inputs[1].wait()
    inputs[2].wait()
    opening = jnp.where(ta == 0, 1.0 / STEP, 0.0)
    for m in range(8):
        b = m % 4
        q = lax.rem(m // 4 + ta, 2)
        planes = [f[8 * b + 2 * g + q] for g in range(4)]
        if m == 0:
            planes[0] = planes[0] + opening * init[...]
        S[pl.ds(m, 128, stride=8), :] = jnp.concatenate(planes, axis=0).T

    pl.semaphore_wait(barrier, len(peers))

    copies_c = []
    for k in range(1, 4):
        to = lax.rem(sx + k, 4)
        q = 4 * (to // 2) + 2 * ta + to % 2
        rows = pl.ds(pl.multiple_of(slice_of(q) * OWN, OWN), OWN)
        c = remote(rsend.at[rows], rrecv.at[sx], c_s.at[k], c_r.at[k],
                   {"sx": to, "sy": sy, "ta": ta})
        c.start()
        copies_c.append(c)
    copies_a = []
    for k in range(1, LINE):
        q = lax.rem(p + k, LINE)
        rows = pl.ds(pl.multiple_of(slice_of(q) * 128, 128), 128)
        c = remote(S.at[rows], rcv.at[p], a_s.at[k], a_r.at[k], in_line(q))
        c.start()
        copies_a.append(c)
    mine = pltpu.make_async_copy(S.at[pl.ds(pl.multiple_of(d * 128, 128), 128)], rcv.at[p],
                                 l_s.at[0])
    mine.start()
    rrecv[sx] = rsend[pl.ds(pl.multiple_of(d * OWN, OWN), OWN), :]
    for c in copies_c:
        c.wait()
    rext[pl.ds(HALO, OWN), :] = (rrecv[0] + rrecv[1]) + (rrecv[2] + rrecv[3])

    def edges(src, left_dst, right_dst, k):
        return (
            remote(src.at[pl.ds(HALO, HALO)], left_dst, h_s.at[2 * k], h_r.at[2 * k], left),
            remote(src.at[pl.ds(OWN, HALO)], right_dst, h_s.at[2 * k + 1], h_r.at[2 * k + 1],
                   right),
        )

    def halos(ref, k):
        return edges(ref, ref.at[pl.ds(ENDS, HALO)], ref.at[pl.ds(0, HALO)], k)

    halo_c = halos(rext, 0)
    for c in halo_c:
        c.start()

    sub = iota(0)
    lane = iota(1)
    first = sub == 0

    def coefficients(cols, inside):
        for col in cols:
            r = jnp.broadcast_to(rext[pl.ds(col, 1), :], (8, 128))
            c = 1.0 / (1.0 / STEP + 4.0 + r)
            cp = c / STEP
            up = (1.0 / STEP + 4.0 + r) * STEP
            q2 = cp * cp
            q4 = q2 * q2
            q = q4 * q4
            qq = q * q
            qqqq = qq * qq
            cl = c * inside
            pw = inside
            for l in range(8):
                CL[col, part(l), :] = cl
                cl = cl * up
                if l:
                    pw = pw * cp
                    PW[col, part(l), :] = pw
            KS[col, part(0), :] = jnp.where(sub < 1, ALPHA * q, q)
            KS[col, part(1), :] = jnp.where(sub < 2, ALPHA * qq, qq)
            KS[col, part(2), :] = jnp.where(sub < 4, ALPHA * qqqq, qqqq)
            ks = inside * cp / (1.0 - ALPHA * (qqqq * qqqq))
            KS[col, part(3), :] = jnp.where(first, ALPHA * ks, ks)

    def solve(g, col):
        v = [g[0]]
        for l in range(1, 8):
            v.append(v[-1] + g[l])
        a = PW[col, part(7), :] * v[7]
        a = a + KS[col, part(0), :] * pltpu.roll(a, 1, 0)
        a = a + KS[col, part(1), :] * pltpu.roll(a, 2, 0)
        a = a + KS[col, part(2), :] * pltpu.roll(a, 4, 0)
        s = KS[col, part(3), :] * pltpu.roll(a, 1, 0)
        return [v[0] + s] + [PW[col, part(l), :] * (v[l] + s) for l in range(1, 8)]

    def rows_beside(v):
        return (jnp.where(lane == 0, 0.0, pltpu.roll(v, 1, 1))
                + jnp.where(lane == 127, 0.0, pltpu.roll(v, 127, 1)))

    def first_sweep(cols):
        done = []
        for col in cols:
            g = []
            for l in range(8):
                g.append(CL[col, part(l), :] * Rx[col, part(l), :])
            done.append((col, g, solve(g, col)))
        for col, g, u in done:
            for l in range(8):
                CR[col, part(l), :] = g[l]
                U0[col, part(l), :] = u[l]

    def around(U, col):
        return [
            (U[col - 1, part(l), :] + U[col + 1, part(l), :]) + rows_beside(U[col, part(l), :])
            for l in range(8)
        ]

    def at_corner(U, col):
        return jnp.where(first, CORNER * pltpu.roll(U[col, part(7), :], 1, 0), 0.0)

    def sweep(src, dst, cols, keep=False):
        done = []
        for col in cols:
            n = around(src, col)
            g = [CR[col, part(l), :] + CL[col, part(l), :] * n[l] for l in range(8)]
            done.append((col, n, solve(g, col)))
        for col, n, u in done:
            for l in range(8):
                dst[col, part(l), :] = u[l]
                if keep:
                    NB[col, part(l), :] = n[l]

    def turning_sweep(src, dst, cols, acc):
        done = []
        for col in cols:
            n = around(src, col)
            e = at_corner(src, col)
            c0 = CR[col, part(0), :] - CL[col, part(0), :] * e
            g = [c0 + CL[col, part(0), :] * n[0]]
            g += [CR[col, part(l), :] + CL[col, part(l), :] * n[l] for l in range(1, 8)]
            for l in range(8):
                r = n[l] - NB[col, part(l), :]
                if l == 0:
                    r = r - e
                acc = acc + r * r
            done.append((col, e, c0, solve(g, col)))
        for col, e, c0, u in done:
            E[col] = e
            CR[col, part(0), :] = c0
            for l in range(8):
                dst[col, part(l), :] = u[l]
        return acc

    def spread(lo, count, fn, carry=0, each=UNROLL):
        def step(i, carry):
            base = lo + each * i
            out = fn([base + k for k in range(each)], carry)
            return carry if out is None else out

        return lax.fori_loop(0, count // each, step, carry)

    spread(HALO, OWN, lambda cols, _: coefficients(cols, 1.0), each=1)
    mine.wait()
    for c in copies_a:
        c.wait()

    def unpack(cols, acc):
        for col in cols:
            rows = pl.ds(pl.multiple_of(8 * col, 8), 8)
            w = []
            for t in range(2):
                v = [rcv[4 * (s // 2) + 2 * t + s % 2, rows, :] for s in range(4)]
                w.append(swap_groups(v))
            for g in range(4):
                even = jnp.where(sub < 4, w[0][g], w[1][g])
                other = pltpu.roll(jnp.where(sub < 4, w[1][g], w[0][g]), 4, 0)
                Rx[HALO + col, part(2 * g), :] = even
                Rx[HALO + col, part(2 * g + 1), :] = other
                acc = acc + even * even + other * other
        return acc

    nothing = jnp.zeros((8, 128), jnp.float32)
    acc0 = spread(0, OWN, unpack, nothing, each=2)
    halo_r = halos(Rx, 1)
    for c in halo_r:
        c.start()
    spread(HALO, OWN, lambda cols, _: first_sweep(cols), each=2)

    def inner(j0, k, src, dst, keep=False):
        sweep(src, dst, [HALO + k + i for i in range(OWN - 2 * k)], keep)

    for i in range(3):
        inner(0, 2 * i + 1, U0, U1)
        inner(0, 2 * i + 2, U1, U0)
    inner(0, 7, U0, U1, True)

    for c in halo_c:
        c.wait()
    at_start = jnp.logical_and(sy == 0, d == 0)
    at_end = jnp.logical_and(sy == nsy - 1, d == 7)
    in_left = jnp.where(at_start, 0.0, 1.0)
    in_right = jnp.where(at_end, 0.0, 1.0)
    spread(0, HALO, lambda cols, _: coefficients(cols, in_left), each=1)
    spread(ENDS, HALO, lambda cols, _: coefficients(cols, in_right), each=1)
    for c in halo_r:
        c.wait()

    def strip(lo, way, src, dst, k, keep=False):
        spread(lo + way * k, HALO, lambda cols, _: sweep(src, dst, cols, keep))

    def strip_a(lo, way, acc):
        spread(0 if way > 0 else ENDS, HALO, lambda cols, _: first_sweep(cols), each=2)

        def pair(i, carry):
            strip(lo, way, U0, U1, 2 * i + 1)
            strip(lo, way, U1, U0, 2 * i + 2)
            return carry

        lax.fori_loop(0, 3, pair, 0)
        strip(lo, way, U0, U1, 7, True)
        return spread(lo + way * 8, HALO, lambda cols, a: turning_sweep(U1, V0, cols, a), acc)

    to_left, to_right = halos(V0, 2)
    e_left, e_right = halos(E, 3)
    acc1 = strip_a(0, 1, nothing)
    to_left.start()
    e_left.start()
    acc1 = strip_a(ENDS, -1, acc1)
    to_right.start()
    e_right.start()

    inner(9, 1, V0, U1)

    for i in range(2):
        inner(9, 2 * i + 2, U1, U0)
        inner(9, 2 * i + 3, U0, U1)
    inner(9, 6, U1, U0)
    inner(9, 7, U0, U1, True)

    def change_rhs(cols, _):
        for col in cols:
            CR[col, part(0), :] = CR[col, part(0), :] - CL[col, part(0), :] * E[col]

    def strip_b(lo, way, outside):
        @pl.when(outside)
        def _():
            def clear(cols, _):
                for col in cols:
                    V0[col] = jnp.zeros((64, 128), jnp.float32)

            spread(0 if way > 0 else ENDS, HALO, clear, each=1)

        spread(0 if way > 0 else ENDS, HALO, change_rhs)
        strip(lo, way, V0, U1, 1)

        def pair(i, carry):
            strip(lo, way, U1, U0, 2 * i + 2)
            strip(lo, way, U0, U1, 2 * i + 3)
            return carry

        lax.fori_loop(0, 2, pair, 0)
        strip(lo, way, U1, U0, 6)
        strip(lo, way, U0, U1, 7, True)

    to_left.wait()
    e_left.wait()
    strip_b(ENDS, -1, at_end)
    to_right.wait()
    e_right.wait()
    strip_b(0, 1, at_start)

    def left_over(cols, acc):
        for col in cols:
            n = around(U1, col)
            for l in range(8):
                r = n[l] - NB[col, part(l), :]
                if l == 0:
                    r = r + (E[col] - at_corner(U1, col))
                acc = acc + r * r
        return acc

    acc2 = spread(HALO, OWN, left_over, nothing, each=2)

    def total(v):
        return jnp.sum(v, axis=0, keepdims=True)

    redx[p] = jnp.where(sub == 0, total(acc0), jnp.where(sub == 1, total(acc1), jnp.where(
        sub == 2, total(acc2), 0.0)))
    copies_x = []
    for k in range(1, LINE):
        c = remote(redx.at[p], redx.at[p], x_s.at[k], x_r.at[k], in_line(lax.rem(p + k, LINE)))
        c.start()
        copies_x.append(c)

    def pack(cols, _):
        for col in cols:
            rows = pl.ds(pl.multiple_of(8 * col, 8), 8)
            w = [[], []]
            for g in range(4):
                even = U1[HALO + col, part(2 * g), :]
                other = pltpu.roll(U1[HALO + col, part(2 * g + 1), :], 4, 0)
                w[0].append(jnp.where(sub < 4, even, other))
                w[1].append(jnp.where(sub < 4, other, even))
            for t in range(2):
                v = swap_groups(w[t])
                for s in range(4):
                    M[4 * (s // 2) + 2 * t + s % 2, rows, :] = v[s]

    spread(0, OWN, pack, each=2)
    slot = pl.ds(pl.multiple_of(d * 128, 128), 128)
    copies_o = []
    for k in range(1, LINE):
        q = lax.rem(p + k, LINE)
        c = remote(M.at[q], O.at[slot], o_s.at[k], o_r.at[k], in_line(q))
        c.start()
        copies_o.append(c)
    mine = pltpu.make_async_copy(M.at[p], O.at[slot], l_s.at[1])
    mine.start()

    for c in copies_x:
        c.wait()
    sums = redx[0]
    for k in range(1, LINE):
        sums = sums + redx[k]
    if ny > 1:
        y = sy // nz
        redy[y] = sums
        copies_y = []
        for k in range(1, ny):
            c = remote(redy.at[y], redy.at[y], y_s.at[k], y_r.at[k], in_y(k))
            c.start()
            copies_y.append(c)
        for c in copies_y:
            c.wait()
        sums = redy[0]
        for k in range(1, ny):
            sums = sums + redy[k]
    if nz > 1:
        z = lax.rem(sy, nz)
        redz[z] = sums
        copies_z = []
        for k in range(1, nz):
            c = remote(redz.at[z], redz.at[z], z_s.at[k], z_r.at[k], in_z(k))
            c.start()
            copies_z.append(c)

    mine.wait()
    for c in copies_o:
        c.wait()
    for m in range(8):
        b = m % 4
        q = lax.rem(m // 4 + ta, 2)
        x = O[pl.ds(m, 128, stride=8), :].T
        for g in range(4):
            out[8 * b + 2 * g + q] = x[32 * g:32 * g + 32, :]

    if nz > 1:
        for c in copies_z:
            c.wait()
        sums = redz[0]
        for k in range(1, nz):
            sums = sums + redz[k]
    cells = 64.0 * 128.0 * (128.0 * nsy)
    for i in range(3):
        stat[i] = jnp.sum(sums[i:i + 1, :]) / cells


def solution(mesh):
    nsy = mesh.shape["sy"]
    ny, nz = (4, 8) if nsy == 32 else (2, nsy // 2)

    def step(forcing, react, initial):
        vmem = pl.BlockSpec(memory_space=pltpu.VMEM)
        dma = pltpu.SemaphoreType.DMA
        f32 = jnp.float32
        return pl.pallas_call(
            functools.partial(kernel, ny, nz),
            out_shape=(
                jax.ShapeDtypeStruct((32, 32, 128), f32),
                jax.ShapeDtypeStruct((3,), f32),
            ),
            in_specs=[pl.BlockSpec(memory_space=pltpu.HBM)] * 3,
            out_specs=(vmem, pl.BlockSpec(memory_space=pltpu.SMEM)),
            scratch_shapes=[
                pltpu.VMEM((32, 32, 128), f32),
                pltpu.VMEM((32, 128), f32),
                pltpu.VMEM((32, 128), f32),
                pltpu.VMEM((1024, 128), f32),
                pltpu.VMEM((8, 128, 128), f32),
                pltpu.VMEM((128, 128), f32),
                pltpu.VMEM((128, 128), f32),
                pltpu.VMEM((4, OWN, 128), f32),
                pltpu.VMEM((WIDE, 128), f32),
            ] + [pltpu.VMEM((WIDE, 64, 128), f32)] * 8 + [
                pltpu.VMEM((WIDE, 32, 128), f32),
                pltpu.VMEM((WIDE, 8, 128), f32),
                pltpu.VMEM((8, 128, 128), f32),
                pltpu.VMEM((1024, 128), f32),
                pltpu.VMEM((LINE, 8, 128), f32),
                pltpu.VMEM((max(ny, 2), 8, 128), f32),
                pltpu.VMEM((max(nz, 2), 8, 128), f32),
                dma((8,)), dma((8,)), dma((4,)), dma((4,)), dma((8,)), dma((8,)),
                dma((8,)), dma((8,)), dma((8,)), dma((8,)), dma((max(ny, 2),)),
                dma((max(ny, 2),)), dma((max(nz, 2),)), dma((max(nz, 2),)), dma((5,)),
            ],
            compiler_params=pltpu.CompilerParams(
                collective_id=0, has_side_effects=True, vmem_limit_bytes=48 << 20
            ),
        )(forcing, react, initial)

    placed = (P("ta", "sx", "sy"), P("sx", "sy"), P("sx", "sy"))
    return jax.shard_map(
        step, mesh=mesh, in_specs=placed, out_specs=(P("ta", "sx", "sy"), P(None)),
        check_vma=False,
    )
```

```python
import functools

import jax
import jax.numpy as jnp
from jax import lax
from jax.experimental import pallas as pl
from jax.experimental.pallas import tpu as pltpu
from jax.sharding import PartitionSpec as P

SWEEPS = 8
ALPHA = 0.1
STEP = 2.0
CORNER = ALPHA / STEP
OWN = 16
HALO = 8
WIDE = OWN + 2 * HALO
ENDS = HALO + OWN
LINE = 8
HUB = LINE - 1
UNROLL = 8
MESH = pl.DeviceIdType.MESH


def iota(axis):
    return lax.broadcasted_iota(jnp.int32, (8, 128), axis)


def place_of(p):
    return 2 * (p // 4) + p % 2, (p // 2) % 2


def swap_groups(v):
    lane = iota(1)
    low = lane < 64
    even = (lane // 32) % 2 == 0
    a = [
        jnp.where(low, v[0], pltpu.roll(v[2], 64, 1)),
        jnp.where(low, v[1], pltpu.roll(v[3], 64, 1)),
        jnp.where(low, pltpu.roll(v[0], 64, 1), v[2]),
        jnp.where(low, pltpu.roll(v[1], 64, 1), v[3]),
    ]
    return [
        jnp.where(even, a[0], pltpu.roll(a[1], 32, 1)),
        jnp.where(even, pltpu.roll(a[0], 96, 1), a[1]),
        jnp.where(even, a[2], pltpu.roll(a[3], 32, 1)),
        jnp.where(even, pltpu.roll(a[2], 96, 1), a[3]),
    ]


def part(l):
    return pl.ds(8 * l, 8)


def kernel(ny, nz, f_hbm, react_hbm, init_hbm, out, stat, f, react, init, S, rcv, tmp, rsend, rrecv,
           rext, Rx, CR, U0, U1, V0, NB, CL, PW, KS, E, M, O, redx, redz, a_s, a_r, c_s, c_r,
           h_s, h_r, o_s, o_r, x_s, x_r, z_s, z_r, l_s, near, far):
    sx, sy, ta = lax.axis_index("sx"), lax.axis_index("sy"), lax.axis_index("ta")
    nsy = ny * nz
    p = 4 * (sx // 2) + 2 * ta + sx % 2
    odd = sy % 2

    def slice_of(q):
        return q + odd * (7 - 2 * q)

    d = slice_of(p)

    def in_line(q):
        a, b = place_of(q)
        return {"sx": a, "sy": sy, "ta": b}

    def beside(step):
        q = d + step
        inside = jnp.logical_and(q >= 0, q <= 7)
        s = jnp.where(inside, sy, lax.rem(sy + step + nsy, nsy))
        e = jnp.where(inside, slice_of(jnp.clip(q, 0, 7)), p)
        a, b = place_of(e)
        return {"sx": a, "sy": s, "ta": b}

    def in_plane(k):
        return {"sx": sx, "sy": lax.rem(sy + k, nsy), "ta": ta}

    left, right = beside(-1), beside(1)
    inputs = [
        pltpu.make_async_copy(react_hbm, react, l_s.at[4]),
        pltpu.make_async_copy(init_hbm, init, l_s.at[5]),
        pltpu.make_async_copy(f_hbm, f, l_s.at[6]),
    ]
    for c in inputs:
        c.start()
    barrier = pltpu.get_barrier_semaphore()
    hub = p == HUB
    for k in range(1, LINE):
        q = lax.rem(p + k, LINE)

        @pl.when(q != HUB)
        def _():
            pl.semaphore_signal(barrier, inc=1, device_id=in_line(q), device_id_type=MESH)

    def remote(src, dst, s_sem, r_sem, peer):
        return pltpu.make_async_remote_copy(
            src_ref=src, dst_ref=dst, send_sem=s_sem, recv_sem=r_sem, device_id=peer,
            device_id_type=MESH,
        )

    tmp[...] = jnp.zeros_like(tmp)
    inputs[0].wait()
    tmp[pl.ds(pl.multiple_of(sx * 32, 32), 32), :] = react[...]
    rsend[...] = tmp[...].T
    inputs[1].wait()
    inputs[2].wait()
    opening = jnp.where(ta == 0, 1.0 / STEP, 0.0)
    for m in range(8):
        b = m % 4
        q = lax.rem(m // 4 + ta, 2)
        planes = [f[8 * b + 2 * g + q] for g in range(4)]
        if m == 0:
            planes[0] = planes[0] + opening * init[...]
        S[pl.ds(m, 128, stride=8), :] = jnp.concatenate(planes, axis=0).T

    @pl.when(jnp.logical_not(hub))
    def _():
        pl.semaphore_wait(barrier, LINE - 1)

    @pl.when(p == HUB - 1)
    def _():
        pl.semaphore_signal(near, inc=1, device_id=in_line(HUB), device_id_type=MESH)

    @pl.when(hub)
    def _():
        pl.semaphore_wait(near, 1)

        def greet(k, carry):
            pl.semaphore_signal(barrier, inc=1, device_id=in_plane(k), device_id_type=MESH)
            return carry

        lax.fori_loop(1, nsy, greet, 0)


    copies_c = []
    for k in range(1, 4):
        to = lax.rem(sx + k, 4)
        q = 4 * (to // 2) + 2 * ta + to % 2
        rows = pl.ds(pl.multiple_of(slice_of(q) * OWN, OWN), OWN)
        c = remote(rsend.at[rows], rrecv.at[sx], c_s.at[k], c_r.at[k],
                   {"sx": to, "sy": sy, "ta": ta})
        c.start()
        copies_c.append(c)
    copies_a = [[], []]
    for h in range(2):
        slots = pl.ds(64 * h, 64)

        def rows_of(q):
            return pl.ds(pl.multiple_of(slice_of(q) * 128 + 64 * h, 64), 64)

        for k in range(1, LINE):
            q = lax.rem(p + k, LINE)
            copies_a[h].append(remote(S.at[rows_of(q)], rcv.at[p, slots], a_s.at[8 * h + k],
                                      a_r.at[8 * h + k], in_line(q)))
        copies_a[h].append(
            pltpu.make_async_copy(S.at[rows_of(p)], rcv.at[p, slots], l_s.at[h]))
        for c in copies_a[h]:
            c.start()
    rrecv[sx] = rsend[pl.ds(pl.multiple_of(d * OWN, OWN), OWN), :]
    for c in copies_c:
        c.wait()
    rext[pl.ds(HALO, OWN), :] = (rrecv[0] + rrecv[1]) + (rrecv[2] + rrecv[3])

    def edges(src, left_dst, right_dst, k):
        return (
            remote(src.at[pl.ds(HALO, HALO)], left_dst, h_s.at[2 * k], h_r.at[2 * k], left),
            remote(src.at[pl.ds(OWN, HALO)], right_dst, h_s.at[2 * k + 1], h_r.at[2 * k + 1],
                   right),
        )

    def halos(ref, k):
        return edges(ref, ref.at[pl.ds(ENDS, HALO)], ref.at[pl.ds(0, HALO)], k)

    halo_c = halos(rext, 0)

    sub = iota(0)
    lane = iota(1)
    first = sub == 0

    def coefficients(cols, inside):
        for col in cols:
            r = jnp.broadcast_to(rext[pl.ds(col, 1), :], (8, 128))
            c = 1.0 / (1.0 / STEP + 4.0 + r)
            cp = c / STEP
            up = (1.0 / STEP + 4.0 + r) * STEP
            q2 = cp * cp
            q4 = q2 * q2
            q = q4 * q4
            qq = q * q
            qqqq = qq * qq
            cl = c * inside
            pw = inside
            for l in range(8):
                CL[col, part(l), :] = cl
                cl = cl * up
                if l:
                    pw = pw * cp
                    PW[col, part(l), :] = pw
            KS[col, part(0), :] = jnp.where(sub < 1, ALPHA * q, q)
            KS[col, part(1), :] = jnp.where(sub < 2, ALPHA * qq, qq)
            KS[col, part(2), :] = jnp.where(sub < 4, ALPHA * qqqq, qqqq)
            ks = inside * cp / (1.0 - ALPHA * (qqqq * qqqq))
            KS[col, part(3), :] = jnp.where(first, ALPHA * ks, ks)

    def solve(g, col):
        v = [g[0]]
        for l in range(1, 8):
            v.append(v[-1] + g[l])
        a = PW[col, part(7), :] * v[7]
        a = a + KS[col, part(0), :] * pltpu.roll(a, 1, 0)
        a = a + KS[col, part(1), :] * pltpu.roll(a, 2, 0)
        a = a + KS[col, part(2), :] * pltpu.roll(a, 4, 0)
        s = KS[col, part(3), :] * pltpu.roll(a, 1, 0)
        return [v[0] + s] + [PW[col, part(l), :] * (v[l] + s) for l in range(1, 8)]

    def rows_beside(v):
        return (jnp.where(lane == 0, 0.0, pltpu.roll(v, 1, 1))
                + jnp.where(lane == 127, 0.0, pltpu.roll(v, 127, 1)))

    def first_sweep(cols):
        done = []
        for col in cols:
            g = []
            for l in range(8):
                g.append(CL[col, part(l), :] * Rx[col, part(l), :])
            done.append((col, g, solve(g, col)))
        for col, g, u in done:
            for l in range(8):
                CR[col, part(l), :] = g[l]
                U0[col, part(l), :] = u[l]

    def around(U, col):
        return [
            (U[col - 1, part(l), :] + U[col + 1, part(l), :]) + rows_beside(U[col, part(l), :])
            for l in range(8)
        ]

    def at_corner(U, col):
        return jnp.where(first, CORNER * pltpu.roll(U[col, part(7), :], 1, 0), 0.0)

    def sweep(src, dst, cols, keep=False):
        done = []
        for col in cols:
            n = around(src, col)
            g = [CR[col, part(l), :] + CL[col, part(l), :] * n[l] for l in range(8)]
            done.append((col, n, solve(g, col)))
        for col, n, u in done:
            for l in range(8):
                dst[col, part(l), :] = u[l]
                if keep:
                    NB[col, part(l), :] = n[l]

    def turning_sweep(src, dst, cols, acc):
        done = []
        for col in cols:
            n = around(src, col)
            e = at_corner(src, col)
            c0 = CR[col, part(0), :] - CL[col, part(0), :] * e
            g = [c0 + CL[col, part(0), :] * n[0]]
            g += [CR[col, part(l), :] + CL[col, part(l), :] * n[l] for l in range(1, 8)]
            for l in range(8):
                r = n[l] - NB[col, part(l), :]
                if l == 0:
                    r = r - e
                acc = acc + r * r
            done.append((col, e, c0, solve(g, col)))
        for col, e, c0, u in done:
            E[col] = e
            CR[col, part(0), :] = c0
            for l in range(8):
                dst[col, part(l), :] = u[l]
        return acc

    def spread(lo, count, fn, carry=0, each=UNROLL):
        def step(i, carry):
            base = lo + each * i
            out = fn([base + k for k in range(each)], carry)
            return carry if out is None else out

        return lax.fori_loop(0, count // each, step, carry)

    spread(HALO, OWN, lambda cols, _: coefficients(cols, 1.0), each=1)

    @pl.when(hub)
    def _():
        pl.semaphore_wait(barrier, nsy - 1)
        for q in range(LINE - 1):
            pl.semaphore_signal(far, inc=1, device_id=in_line(q), device_id_type=MESH)


    def unpack(cols, acc):
        for col in cols:
            rows = pl.ds(pl.multiple_of(8 * col, 8), 8)
            w = []
            for t in range(2):
                v = [rcv[4 * (s // 2) + 2 * t + s % 2, rows, :] for s in range(4)]
                w.append(swap_groups(v))
            for g in range(4):
                even = jnp.where(sub < 4, w[0][g], w[1][g])
                other = pltpu.roll(jnp.where(sub < 4, w[1][g], w[0][g]), 4, 0)
                Rx[HALO + col, part(2 * g), :] = even
                Rx[HALO + col, part(2 * g + 1), :] = other
                acc = acc + even * even + other * other
        return acc

    nothing = jnp.zeros((8, 128), jnp.float32)
    halo_r = halos(Rx, 1)
    acc0 = nothing
    for h in range(2):
        for c in copies_a[h]:
            c.wait()
        acc0 = spread(HALO * h, HALO, unpack, acc0, each=2)
        if h == 0:
            @pl.when(jnp.logical_not(hub))
            def _():
                pl.semaphore_wait(far, 1)

            for c in halo_c:
                c.start()
        halo_r[h].start()
    spread(HALO, OWN, lambda cols, _: first_sweep(cols), each=2)

    def inner(j0, k, src, dst, keep=False):
        sweep(src, dst, [HALO + k + i for i in range(OWN - 2 * k)], keep)

    for i in range(3):
        inner(0, 2 * i + 1, U0, U1)
        inner(0, 2 * i + 2, U1, U0)
    inner(0, 7, U0, U1, True)

    for c in halo_c:
        c.wait()
    at_start = jnp.logical_and(sy == 0, d == 0)
    at_end = jnp.logical_and(sy == nsy - 1, d == 7)
    in_left = jnp.where(at_start, 0.0, 1.0)
    in_right = jnp.where(at_end, 0.0, 1.0)
    spread(0, HALO, lambda cols, _: coefficients(cols, in_left), each=1)
    spread(ENDS, HALO, lambda cols, _: coefficients(cols, in_right), each=1)
    for c in halo_r:
        c.wait()

    def strip(lo, way, src, dst, k, keep=False):
        spread(lo + way * k, HALO, lambda cols, _: sweep(src, dst, cols, keep))

    def strip_a(lo, way, acc):
        spread(0 if way > 0 else ENDS, HALO, lambda cols, _: first_sweep(cols), each=2)

        def pair(i, carry):
            strip(lo, way, U0, U1, 2 * i + 1)
            strip(lo, way, U1, U0, 2 * i + 2)
            return carry

        lax.fori_loop(0, 3, pair, 0)
        strip(lo, way, U0, U1, 7, True)
        return spread(lo + way * 8, HALO, lambda cols, a: turning_sweep(U1, V0, cols, a), acc)

    to_left, to_right = halos(V0, 2)
    e_left, e_right = halos(E, 3)
    acc1 = strip_a(0, 1, nothing)
    to_left.start()
    e_left.start()
    acc1 = strip_a(ENDS, -1, acc1)
    to_right.start()
    e_right.start()

    inner(9, 1, V0, U1)

    for i in range(2):
        inner(9, 2 * i + 2, U1, U0)
        inner(9, 2 * i + 3, U0, U1)
    inner(9, 6, U1, U0)
    inner(9, 7, U0, U1, True)

    def change_rhs(cols, _):
        for col in cols:
            CR[col, part(0), :] = CR[col, part(0), :] - CL[col, part(0), :] * E[col]

    def strip_b(lo, way, outside):
        @pl.when(outside)
        def _():
            def clear(cols, _):
                for col in cols:
                    V0[col] = jnp.zeros((64, 128), jnp.float32)

            spread(0 if way > 0 else ENDS, HALO, clear, each=1)

        spread(0 if way > 0 else ENDS, HALO, change_rhs)
        strip(lo, way, V0, U1, 1)

        def pair(i, carry):
            strip(lo, way, U1, U0, 2 * i + 2)
            strip(lo, way, U0, U1, 2 * i + 3)
            return carry

        lax.fori_loop(0, 2, pair, 0)
        strip(lo, way, U1, U0, 6)
        strip(lo, way, U0, U1, 7, True)

    def left_over(cols, acc):
        for col in cols:
            n = around(U1, col)
            for l in range(8):
                r = n[l] - NB[col, part(l), :]
                if l == 0:
                    r = r + (E[col] - at_corner(U1, col))
                acc = acc + r * r
        return acc


    def pack(cols, _):
        for col in cols:
            rows = pl.ds(pl.multiple_of(8 * col, 8), 8)
            w = [[], []]
            for g in range(4):
                even = U1[HALO + col, part(2 * g), :]
                other = pltpu.roll(U1[HALO + col, part(2 * g + 1), :], 4, 0)
                w[0].append(jnp.where(sub < 4, even, other))
                w[1].append(jnp.where(sub < 4, other, even))
            for t in range(2):
                v = swap_groups(w[t])
                for s in range(4):
                    M[4 * (s // 2) + 2 * t + s % 2, rows, :] = v[s]

    copies_o = []

    def send_out(h):
        slot = pl.ds(pl.multiple_of(d * 128 + 64 * h, 64), 64)
        rows = pl.ds(64 * h, 64)
        for k in range(1, LINE):
            q = lax.rem(p + k, LINE)
            copies_o.append(remote(M.at[q, rows], O.at[slot], o_s.at[8 * h + k],
                                   o_r.at[8 * h + k], in_line(q)))
            copies_o[-1].start()
        copies_o.append(pltpu.make_async_copy(M.at[p, rows], O.at[slot], l_s.at[2 + h]))
        copies_o[-1].start()

    to_left.wait()
    e_left.wait()
    strip_b(ENDS, -1, at_end)
    acc2 = spread(HALO + OWN // 2, OWN // 2, left_over, nothing, each=4)
    spread(OWN // 2, OWN // 2, pack, each=2)
    send_out(1)
    to_right.wait()
    e_right.wait()
    strip_b(0, 1, at_start)
    acc2 = spread(HALO, OWN // 2, left_over, acc2, each=4)

    def total(v):
        return jnp.sum(v, axis=0, keepdims=True)

    redx[p] = jnp.where(sub == 0, total(acc0), jnp.where(sub == 1, total(acc1), jnp.where(
        sub == 2, total(acc2), 0.0)))
    copies_x = []
    for k in range(1, LINE):
        c = remote(redx.at[p], redx.at[p], x_s.at[k], x_r.at[k], in_line(lax.rem(p + k, LINE)))
        c.start()
        copies_x.append(c)

    spread(0, OWN // 2, pack, each=2)
    send_out(0)
    for c in copies_x:
        c.wait()
    sums = redx[0]
    for k in range(1, LINE):
        sums = sums + redx[k]
    redz[sy] = sums

    def plane(k):
        return remote(redz.at[sy], redz.at[sy], z_s.at[k], z_r.at[k], in_plane(k))

    def send(k, carry):
        plane(k).start()
        return carry

    lax.fori_loop(1, nsy, send, 0)

    for c in copies_o:
        c.wait()
    for m in range(8):
        b = m % 4
        q = lax.rem(m // 4 + ta, 2)
        x = O[pl.ds(m, 128, stride=8), :].T
        for g in range(4):
            out[8 * b + 2 * g + q] = x[32 * g:32 * g + 32, :]

    def arrive(k, carry):
        plane(k).wait()
        return carry

    lax.fori_loop(1, nsy, arrive, 0)
    sums = redz[0]
    for k in range(1, nsy):
        sums = sums + redz[k]
    cells = 64.0 * 128.0 * (128.0 * nsy)
    for i in range(3):
        stat[i] = jnp.sum(sums[i:i + 1, :]) / cells


def solution(mesh):
    nsy = mesh.shape["sy"]
    ny, nz = (4, 8) if nsy == 32 else (2, nsy // 2)

    def step(forcing, react, initial):
        vmem = pl.BlockSpec(memory_space=pltpu.VMEM)
        dma = pltpu.SemaphoreType.DMA
        f32 = jnp.float32
        return pl.pallas_call(
            functools.partial(kernel, ny, nz),
            out_shape=(
                jax.ShapeDtypeStruct((32, 32, 128), f32),
                jax.ShapeDtypeStruct((3,), f32),
            ),
            in_specs=[pl.BlockSpec(memory_space=pltpu.HBM)] * 3,
            out_specs=(vmem, pl.BlockSpec(memory_space=pltpu.SMEM)),
            scratch_shapes=[
                pltpu.VMEM((32, 32, 128), f32),
                pltpu.VMEM((32, 128), f32),
                pltpu.VMEM((32, 128), f32),
                pltpu.VMEM((1024, 128), f32),
                pltpu.VMEM((8, 128, 128), f32),
                pltpu.VMEM((128, 128), f32),
                pltpu.VMEM((128, 128), f32),
                pltpu.VMEM((4, OWN, 128), f32),
                pltpu.VMEM((WIDE, 128), f32),
            ] + [pltpu.VMEM((WIDE, 64, 128), f32)] * 8 + [
                pltpu.VMEM((WIDE, 32, 128), f32),
                pltpu.VMEM((WIDE, 8, 128), f32),
                pltpu.VMEM((8, 128, 128), f32),
                pltpu.VMEM((1024, 128), f32),
                pltpu.VMEM((LINE, 8, 128), f32),
                pltpu.VMEM((ny * nz, 8, 128), f32),
                dma((16,)), dma((16,)), dma((4,)), dma((4,)), dma((8,)), dma((8,)),
                dma((16,)), dma((16,)), dma((8,)), dma((8,)),
                dma((ny * nz,)), dma((ny * nz,)), dma((7,)),
                pltpu.SemaphoreType.REGULAR, pltpu.SemaphoreType.REGULAR,
            ],
            compiler_params=pltpu.CompilerParams(
                collective_id=0, has_side_effects=True, vmem_limit_bytes=67043328
            ),
        )(forcing, react, initial)

    placed = (P("ta", "sx", "sy"), P("sx", "sy"), P("sx", "sy"))
    return jax.shard_map(
        step, mesh=mesh, in_specs=placed, out_specs=(P("ta", "sx", "sy"), P(None)),
        check_vma=False,
    )
```

```python
import functools

import jax
import jax.numpy as jnp
from jax import lax
from jax.experimental import pallas as pl
from jax.experimental.pallas import tpu as pltpu
from jax.sharding import PartitionSpec as P

SWEEPS = 8
ALPHA = 0.1
STEP = 2.0
CORNER = ALPHA / STEP
OWN = 16
HALO = 8
WIDE = OWN + 2 * HALO
ENDS = HALO + OWN
LINE = 8
HUB = LINE - 1
UNROLL = 8
TURN_VMEM = 67043328
MESH = pl.DeviceIdType.MESH


def iota(axis):
    return lax.broadcasted_iota(jnp.int32, (8, 128), axis)


def place_of(p):
    return 2 * (p // 4) + p % 2, (p // 2) % 2


def swap_groups(v):
    lane = iota(1)
    low = lane < 64
    even = (lane // 32) % 2 == 0

    def cross(a, b):
        y = pltpu.roll(jnp.where(low, b, a), 64, 1)
        return jnp.where(low, a, y), jnp.where(low, y, b)

    a0, a2 = cross(v[0], v[2])
    a1, a3 = cross(v[1], v[3])
    a = [a0, a1, a2, a3]
    return [
        jnp.where(even, a[0], pltpu.roll(a[1], 32, 1)),
        jnp.where(even, pltpu.roll(a[0], 96, 1), a[1]),
        jnp.where(even, a[2], pltpu.roll(a[3], 32, 1)),
        jnp.where(even, pltpu.roll(a[2], 96, 1), a[3]),
    ]


def part(l):
    return pl.ds(8 * l, 8)


def kernel(ny, nz, f_hbm, react_hbm, init_hbm, O, stat, f, react, init, S, rcv, tmp, rsend, rrecv,
           rext, Rx, CR, U0, U1, V0, NB, CL, PW, KS, E, M, redx, redz, a_s, a_r, c_s, c_r,
           h_s, h_r, o_s, o_r, x_s, x_r, z_s, z_r, l_s, near, far):
    sx, sy, ta = lax.axis_index("sx"), lax.axis_index("sy"), lax.axis_index("ta")
    nsy = ny * nz
    p = 4 * (sx // 2) + 2 * ta + sx % 2
    odd = sy % 2

    def slice_of(q):
        return q + odd * (7 - 2 * q)

    d = slice_of(p)

    def in_line(q):
        a, b = place_of(q)
        return {"sx": a, "sy": sy, "ta": b}

    def beside(step):
        q = d + step
        inside = jnp.logical_and(q >= 0, q <= 7)
        s = jnp.where(inside, sy, lax.rem(sy + step + nsy, nsy))
        e = jnp.where(inside, slice_of(jnp.clip(q, 0, 7)), p)
        a, b = place_of(e)
        return {"sx": a, "sy": s, "ta": b}

    def in_plane(k):
        return {"sx": sx, "sy": lax.rem(sy + k, nsy), "ta": ta}

    left, right = beside(-1), beside(1)
    inputs = [
        pltpu.make_async_copy(react_hbm, react, l_s.at[4]),
        pltpu.make_async_copy(init_hbm, init, l_s.at[5]),
        pltpu.make_async_copy(f_hbm, f, l_s.at[6]),
    ]
    for c in inputs:
        c.start()
    barrier = pltpu.get_barrier_semaphore()
    hub = p == HUB
    for k in range(1, LINE):
        q = lax.rem(p + k, LINE)

        @pl.when(q != HUB)
        def _():
            pl.semaphore_signal(barrier, inc=1, device_id=in_line(q), device_id_type=MESH)

    def remote(src, dst, s_sem, r_sem, peer):
        return pltpu.make_async_remote_copy(
            src_ref=src, dst_ref=dst, send_sem=s_sem, recv_sem=r_sem, device_id=peer,
            device_id_type=MESH,
        )

    tmp[...] = jnp.zeros_like(tmp)
    inputs[0].wait()
    tmp[pl.ds(pl.multiple_of(sx * 32, 32), 32), :] = react[...]
    rsend[...] = tmp[...].T
    inputs[1].wait()
    inputs[2].wait()
    opening = jnp.where(ta == 0, 1.0 / STEP, 0.0)
    for m in range(8):
        b = m % 4
        q = lax.rem(m // 4 + ta, 2)
        planes = [f[8 * b + 2 * g + q] for g in range(4)]
        if m == 0:
            planes[0] = planes[0] + opening * init[...]
        S[pl.ds(m, 128, stride=8), :] = jnp.concatenate(planes, axis=0).T

    @pl.when(jnp.logical_not(hub))
    def _():
        pl.semaphore_wait(barrier, LINE - 1)

    @pl.when(p == HUB - 1)
    def _():
        pl.semaphore_signal(near, inc=1, device_id=in_line(HUB), device_id_type=MESH)

    @pl.when(hub)
    def _():
        pl.semaphore_wait(near, 1)

        def greet(k, carry):
            pl.semaphore_signal(barrier, inc=1, device_id=in_plane(k), device_id_type=MESH)
            return carry

        lax.fori_loop(1, nsy, greet, 0)


    copies_c = []
    for k in range(1, 4):
        to = lax.rem(sx + k, 4)
        q = 4 * (to // 2) + 2 * ta + to % 2
        rows = pl.ds(pl.multiple_of(slice_of(q) * OWN, OWN), OWN)
        c = remote(rsend.at[rows], rrecv.at[sx], c_s.at[k], c_r.at[k],
                   {"sx": to, "sy": sy, "ta": ta})
        c.start()
        copies_c.append(c)
    copies_a = [[], []]
    for h in range(2):
        slots = pl.ds(64 * h, 64)

        def rows_of(q):
            return pl.ds(pl.multiple_of(slice_of(q) * 128 + 64 * h, 64), 64)

        for k in range(1, LINE):
            q = lax.rem(p + k, LINE)
            copies_a[h].append(remote(S.at[rows_of(q)], rcv.at[p, slots], a_s.at[8 * h + k],
                                      a_r.at[8 * h + k], in_line(q)))
        copies_a[h].append(
            pltpu.make_async_copy(S.at[rows_of(p)], rcv.at[p, slots], l_s.at[h]))
        for c in copies_a[h]:
            c.start()
    rrecv[sx] = rsend[pl.ds(pl.multiple_of(d * OWN, OWN), OWN), :]
    for c in copies_c:
        c.wait()
    rext[pl.ds(HALO, OWN), :] = (rrecv[0] + rrecv[1]) + (rrecv[2] + rrecv[3])

    def edges(src, left_dst, right_dst, k):
        return (
            remote(src.at[pl.ds(HALO, HALO)], left_dst, h_s.at[2 * k], h_r.at[2 * k], left),
            remote(src.at[pl.ds(OWN, HALO)], right_dst, h_s.at[2 * k + 1], h_r.at[2 * k + 1],
                   right),
        )

    def halos(ref, k):
        return edges(ref, ref.at[pl.ds(ENDS, HALO)], ref.at[pl.ds(0, HALO)], k)

    halo_c = halos(rext, 0)

    sub = iota(0)
    lane = iota(1)
    first = sub == 0

    def coefficients(cols, inside):
        for col in cols:
            r = jnp.broadcast_to(rext[pl.ds(col, 1), :], (8, 128))
            c = 1.0 / (1.0 / STEP + 4.0 + r)
            cp = c / STEP
            up = (1.0 / STEP + 4.0 + r) * STEP
            q2 = cp * cp
            q4 = q2 * q2
            q = q4 * q4
            qq = q * q
            qqqq = qq * qq
            cl = c * inside
            pw = inside
            for l in range(8):
                CL[col, part(l), :] = cl
                cl = cl * up
                if l:
                    pw = pw * cp
                    PW[col, part(l), :] = pw
            KS[col, part(0), :] = jnp.where(sub < 1, ALPHA * q, q)
            KS[col, part(1), :] = jnp.where(sub < 2, ALPHA * qq, qq)
            KS[col, part(2), :] = jnp.where(sub < 4, ALPHA * qqqq, qqqq)
            ks = inside * cp / (1.0 - ALPHA * (qqqq * qqqq))
            KS[col, part(3), :] = jnp.where(first, ALPHA * ks, ks)

    def solve(g, col):
        v = [g[0]]
        for l in range(1, 8):
            v.append(v[-1] + g[l])
        a = PW[col, part(7), :] * v[7]
        a = a + KS[col, part(0), :] * pltpu.roll(a, 1, 0)
        a = a + KS[col, part(1), :] * pltpu.roll(a, 2, 0)
        a = a + KS[col, part(2), :] * pltpu.roll(a, 4, 0)
        s = KS[col, part(3), :] * pltpu.roll(a, 1, 0)
        return [v[0] + s] + [PW[col, part(l), :] * (v[l] + s) for l in range(1, 8)]

    def rows_beside(v):
        return (jnp.where(lane == 0, 0.0, pltpu.roll(v, 1, 1))
                + jnp.where(lane == 127, 0.0, pltpu.roll(v, 127, 1)))

    def first_sweep(cols):
        done = []
        for col in cols:
            g = []
            for l in range(8):
                g.append(CL[col, part(l), :] * Rx[col, part(l), :])
            done.append((col, g, solve(g, col)))
        for col, g, u in done:
            for l in range(8):
                CR[col, part(l), :] = g[l]
                U0[col, part(l), :] = u[l]

    def around(U, col):
        return [
            (U[col - 1, part(l), :] + U[col + 1, part(l), :]) + rows_beside(U[col, part(l), :])
            for l in range(8)
        ]

    def at_corner(U, col):
        return jnp.where(first, CORNER * pltpu.roll(U[col, part(7), :], 1, 0), 0.0)

    def sweep(src, dst, cols, keep=False):
        done = []
        for col in cols:
            n = around(src, col)
            g = [CR[col, part(l), :] + CL[col, part(l), :] * n[l] for l in range(8)]
            done.append((col, n, solve(g, col)))
        for col, n, u in done:
            for l in range(8):
                dst[col, part(l), :] = u[l]
                if keep:
                    NB[col, part(l), :] = n[l]

    def turning_sweep(src, dst, cols, acc):
        done = []
        for col in cols:
            n = around(src, col)
            e = at_corner(src, col)
            c0 = CR[col, part(0), :] - CL[col, part(0), :] * e
            g = [c0 + CL[col, part(0), :] * n[0]]
            g += [CR[col, part(l), :] + CL[col, part(l), :] * n[l] for l in range(1, 8)]
            for l in range(8):
                r = n[l] - NB[col, part(l), :]
                if l == 0:
                    r = r - e
                acc = acc + r * r
            done.append((col, e, c0, solve(g, col)))
        for col, e, c0, u in done:
            E[col] = e
            CR[col, part(0), :] = c0
            for l in range(8):
                dst[col, part(l), :] = u[l]
        return acc

    def spread(lo, count, fn, carry=0, each=UNROLL):
        def step(i, carry):
            base = lo + each * i
            out = fn([base + k for k in range(each)], carry)
            return carry if out is None else out

        return lax.fori_loop(0, count // each, step, carry)

    spread(HALO, OWN, lambda cols, _: coefficients(cols, 1.0), each=1)

    @pl.when(hub)
    def _():
        pl.semaphore_wait(barrier, nsy - 1)
        for q in range(LINE - 1):
            pl.semaphore_signal(far, inc=1, device_id=in_line(q), device_id_type=MESH)


    def unpack(cols, acc):
        for col in cols:
            rows = pl.ds(pl.multiple_of(8 * col, 8), 8)
            w = []
            for t in range(2):
                v = [rcv[4 * (s // 2) + 2 * t + s % 2, rows, :] for s in range(4)]
                w.append(swap_groups(v))
            for g in range(4):
                even = jnp.where(sub < 4, w[0][g], w[1][g])
                other = pltpu.roll(jnp.where(sub < 4, w[1][g], w[0][g]), 4, 0)
                Rx[HALO + col, part(2 * g), :] = even
                Rx[HALO + col, part(2 * g + 1), :] = other
                acc = acc + even * even + other * other
        return acc

    nothing = jnp.zeros((8, 128), jnp.float32)
    halo_r = halos(Rx, 1)
    acc0 = nothing
    for h in range(2):
        for c in copies_a[h]:
            c.wait()
        acc0 = spread(HALO * h, HALO, unpack, acc0, each=2)
        if h == 0:
            @pl.when(jnp.logical_not(hub))
            def _():
                pl.semaphore_wait(far, 1)

            for c in halo_c:
                c.start()
        halo_r[h].start()
    spread(HALO, OWN, lambda cols, _: first_sweep(cols), each=2)

    def inner(j0, k, src, dst, keep=False):
        sweep(src, dst, [HALO + k + i for i in range(OWN - 2 * k)], keep)

    for i in range(3):
        inner(0, 2 * i + 1, U0, U1)
        inner(0, 2 * i + 2, U1, U0)
    inner(0, 7, U0, U1, True)

    at_start = jnp.logical_and(sy == 0, d == 0)
    at_end = jnp.logical_and(sy == nsy - 1, d == 7)
    in_left = jnp.where(at_start, 0.0, 1.0)
    in_right = jnp.where(at_end, 0.0, 1.0)

    def strip(lo, way, src, dst, k, keep=False):
        spread(lo + way * k, HALO, lambda cols, _: sweep(src, dst, cols, keep))

    def strip_a(lo, way, acc):
        spread(0 if way > 0 else ENDS, HALO, lambda cols, _: first_sweep(cols), each=2)

        def pair(i, carry):
            strip(lo, way, U0, U1, 2 * i + 1)
            strip(lo, way, U1, U0, 2 * i + 2)
            return carry

        lax.fori_loop(0, 3, pair, 0)
        strip(lo, way, U0, U1, 7, True)
        return spread(lo + way * 8, HALO, lambda cols, a: turning_sweep(U1, V0, cols, a), acc)

    to_left, to_right = halos(V0, 2)
    e_left, e_right = halos(E, 3)
    halo_c[0].wait()
    spread(ENDS, HALO, lambda cols, _: coefficients(cols, in_right), each=1)
    halo_r[0].wait()
    acc1 = strip_a(ENDS, -1, nothing)
    to_right.start()
    e_right.start()
    halo_c[1].wait()
    spread(0, HALO, lambda cols, _: coefficients(cols, in_left), each=1)
    halo_r[1].wait()
    acc1 = strip_a(0, 1, acc1)
    to_left.start()
    e_left.start()

    inner(9, 1, V0, U1)

    for i in range(2):
        inner(9, 2 * i + 2, U1, U0)
        inner(9, 2 * i + 3, U0, U1)
    inner(9, 6, U1, U0)
    inner(9, 7, U0, U1, True)

    def change_rhs(cols, _):
        for col in cols:
            CR[col, part(0), :] = CR[col, part(0), :] - CL[col, part(0), :] * E[col]

    def strip_b(lo, way, outside):
        @pl.when(outside)
        def _():
            def clear(cols, _):
                for col in cols:
                    V0[col] = jnp.zeros((64, 128), jnp.float32)

            spread(0 if way > 0 else ENDS, HALO, clear, each=1)

        spread(0 if way > 0 else ENDS, HALO, change_rhs)
        strip(lo, way, V0, U1, 1)

        def pair(i, carry):
            strip(lo, way, U1, U0, 2 * i + 2)
            strip(lo, way, U0, U1, 2 * i + 3)
            return carry

        lax.fori_loop(0, 2, pair, 0)
        strip(lo, way, U1, U0, 6)
        strip(lo, way, U0, U1, 7, True)

    def left_over(cols, acc):
        for col in cols:
            n = around(U1, col)
            for l in range(8):
                r = n[l] - NB[col, part(l), :]
                if l == 0:
                    r = r + (E[col] - at_corner(U1, col))
                acc = acc + r * r
        return acc


    def pack(cols, _):
        for col in cols:
            rows = pl.ds(pl.multiple_of(8 * col, 8), 8)
            w = [[], []]
            for g in range(4):
                even = U1[HALO + col, part(2 * g), :]
                other = pltpu.roll(U1[HALO + col, part(2 * g + 1), :], 4, 0)
                w[0].append(jnp.where(sub < 4, even, other))
                w[1].append(jnp.where(sub < 4, other, even))
            for t in range(2):
                v = swap_groups(w[t])
                for s in range(4):
                    M[4 * (s // 2) + 2 * t + s % 2, rows, :] = v[s]

    copies_o = []

    def send_out(h):
        slot = pl.ds(pl.multiple_of(d * 128 + 64 * h, 64), 64)
        rows = pl.ds(64 * h, 64)
        for k in range(1, LINE):
            q = lax.rem(p + k, LINE)
            copies_o.append(remote(M.at[q, rows], O.at[slot], o_s.at[8 * h + k],
                                   o_r.at[8 * h + k], in_line(q)))
            copies_o[-1].start()
        copies_o.append(pltpu.make_async_copy(M.at[p, rows], O.at[slot], l_s.at[2 + h]))
        copies_o[-1].start()

    to_right.wait()
    e_right.wait()
    strip_b(0, 1, at_start)
    acc2 = spread(HALO, OWN // 2, left_over, nothing, each=4)
    spread(0, OWN // 2, pack, each=2)
    send_out(0)
    to_left.wait()
    e_left.wait()
    strip_b(ENDS, -1, at_end)
    acc2 = spread(HALO + OWN // 2, OWN // 2, left_over, acc2, each=4)

    def total(v):
        return jnp.sum(v, axis=0, keepdims=True)

    redx[p] = jnp.where(sub == 0, total(acc0), jnp.where(sub == 1, total(acc1), jnp.where(
        sub == 2, total(acc2), 0.0)))
    copies_x = []
    for k in range(1, LINE):
        c = remote(redx.at[p], redx.at[p], x_s.at[k], x_r.at[k], in_line(lax.rem(p + k, LINE)))
        c.start()
        copies_x.append(c)

    spread(OWN // 2, OWN // 2, pack, each=2)
    send_out(1)
    for c in copies_x:
        c.wait()
    sums = redx[0]
    for k in range(1, LINE):
        sums = sums + redx[k]
    redz[sy] = sums

    def plane(k):
        return remote(redz.at[sy], redz.at[sy], z_s.at[k], z_r.at[k], in_plane(k))

    def send(k, carry):
        plane(k).start()
        return carry

    lax.fori_loop(1, nsy, send, 0)

    for c in copies_o:
        c.wait()
    def arrive(k, carry):
        plane(k).wait()
        return carry

    lax.fori_loop(1, nsy, arrive, 0)
    sums = redz[0]
    for k in range(1, nsy):
        sums = sums + redz[k]
    stat[...] = sums


def turn(cells, turned, sums, out, stat):
    ta = lax.axis_index("ta")
    for m in range(8):
        b = m % 4
        q = lax.rem(m // 4 + ta, 2)
        x = turned[pl.ds(m, 128, stride=8), :].T
        for g in range(4):
            out[8 * b + 2 * g + q] = x[32 * g:32 * g + 32, :]
    for i in range(3):
        stat[i] = jnp.sum(sums[i:i + 1, :]) / cells


def solution(mesh):
    nsy = mesh.shape["sy"]
    ny, nz = (4, 8) if nsy == 32 else (2, nsy // 2)

    def step(forcing, react, initial):
        vmem = pl.BlockSpec(memory_space=pltpu.VMEM)
        dma = pltpu.SemaphoreType.DMA
        f32 = jnp.float32
        turned, sums = pl.pallas_call(
            functools.partial(kernel, ny, nz),
            out_shape=(
                jax.ShapeDtypeStruct((1024, 128), f32),
                jax.ShapeDtypeStruct((8, 128), f32),
            ),
            in_specs=[pl.BlockSpec(memory_space=pltpu.HBM)] * 3,
            out_specs=(pl.BlockSpec(memory_space=pltpu.HBM), vmem),
            scratch_shapes=[
                pltpu.VMEM((32, 32, 128), f32),
                pltpu.VMEM((32, 128), f32),
                pltpu.VMEM((32, 128), f32),
                pltpu.VMEM((1024, 128), f32),
                pltpu.VMEM((8, 128, 128), f32),
                pltpu.VMEM((128, 128), f32),
                pltpu.VMEM((128, 128), f32),
                pltpu.VMEM((4, OWN, 128), f32),
                pltpu.VMEM((WIDE, 128), f32),
            ] + [pltpu.VMEM((WIDE, 64, 128), f32)] * 8 + [
                pltpu.VMEM((WIDE, 32, 128), f32),
                pltpu.VMEM((WIDE, 8, 128), f32),
                pltpu.VMEM((8, 128, 128), f32),
                pltpu.VMEM((LINE, 8, 128), f32),
                pltpu.VMEM((ny * nz, 8, 128), f32),
                dma((16,)), dma((16,)), dma((4,)), dma((4,)), dma((8,)), dma((8,)),
                dma((16,)), dma((16,)), dma((8,)), dma((8,)),
                dma((ny * nz,)), dma((ny * nz,)), dma((7,)),
                pltpu.SemaphoreType.REGULAR, pltpu.SemaphoreType.REGULAR,
            ],
            compiler_params=pltpu.CompilerParams(
                collective_id=0, has_side_effects=True, vmem_limit_bytes=67043328
            ),
        )(forcing, react, initial)
        return pl.pallas_call(
            functools.partial(turn, 64.0 * 128.0 * 128.0 * nsy),
            out_shape=(
                jax.ShapeDtypeStruct((32, 32, 128), f32),
                jax.ShapeDtypeStruct((3,), f32),
            ),
            in_specs=[vmem] * 2,
            out_specs=(vmem, pl.BlockSpec(memory_space=pltpu.SMEM)),
            compiler_params=pltpu.CompilerParams(vmem_limit_bytes=TURN_VMEM),
        )(turned, sums)

    placed = (P("ta", "sx", "sy"), P("sx", "sy"), P("sx", "sy"))
    return jax.shard_map(
        step, mesh=mesh, in_specs=placed, out_specs=(P("ta", "sx", "sy"), P(None)),
        check_vma=False,
    )
```

```python
import functools

import jax
import jax.numpy as jnp
from jax import lax
from jax.experimental import pallas as pl
from jax.experimental.pallas import tpu as pltpu
from jax.sharding import PartitionSpec as P

SWEEPS = 8
ALPHA = 0.1
STEP = 2.0
CORNER = ALPHA / STEP
OWN = 16
HALO = 8
WIDE = OWN + 2 * HALO
ENDS = HALO + OWN
LINE = 8
HUB = LINE - 1
UNROLL = 8
TURN_VMEM = 67043328
MESH = pl.DeviceIdType.MESH


def iota(axis):
    return lax.broadcasted_iota(jnp.int32, (8, 128), axis)


def place_of(p):
    return 2 * (p // 4) + p % 2, (p // 2) % 2


def swap_groups(v):
    lane = iota(1)
    low = lane < 64
    even = (lane // 32) % 2 == 0

    def cross(a, b):
        y = pltpu.roll(jnp.where(low, b, a), 64, 1)
        return jnp.where(low, a, y), jnp.where(low, y, b)

    a0, a2 = cross(v[0], v[2])
    a1, a3 = cross(v[1], v[3])
    a = [a0, a1, a2, a3]
    return [
        jnp.where(even, a[0], pltpu.roll(a[1], 32, 1)),
        jnp.where(even, pltpu.roll(a[0], 96, 1), a[1]),
        jnp.where(even, a[2], pltpu.roll(a[3], 32, 1)),
        jnp.where(even, pltpu.roll(a[2], 96, 1), a[3]),
    ]


def part(l):
    return pl.ds(8 * l, 8)


def kernel(ny, nz, f_hbm, react_hbm, init_hbm, O, stat, f, react, init, S, rcv, tmp, rsend, rrecv,
           rext, Rx, CR, U0, U1, V0, NB, CL, PW, KS, E, M, redx, redz, a_s, a_r, c_s, c_r,
           h_s, h_r, o_s, o_r, x_s, x_r, z_s, z_r, l_s, near, far):
    sx, sy, ta = lax.axis_index("sx"), lax.axis_index("sy"), lax.axis_index("ta")
    nsy = ny * nz
    p = 4 * (sx // 2) + 2 * ta + sx % 2
    odd = sy % 2

    def slice_of(q):
        return q + odd * (7 - 2 * q)

    d = slice_of(p)

    def in_line(q):
        a, b = place_of(q)
        return {"sx": a, "sy": sy, "ta": b}

    def beside(step):
        q = d + step
        inside = jnp.logical_and(q >= 0, q <= 7)
        s = jnp.where(inside, sy, lax.rem(sy + step + nsy, nsy))
        e = jnp.where(inside, slice_of(jnp.clip(q, 0, 7)), p)
        a, b = place_of(e)
        return {"sx": a, "sy": s, "ta": b}

    def in_plane(k):
        return {"sx": sx, "sy": lax.rem(sy + k, nsy), "ta": ta}

    left, right = beside(-1), beside(1)
    inputs = [
        pltpu.make_async_copy(react_hbm, react, l_s.at[4]),
        pltpu.make_async_copy(init_hbm, init, l_s.at[5]),
        pltpu.make_async_copy(f_hbm, f, l_s.at[6]),
    ]
    for c in inputs:
        c.start()
    barrier = pltpu.get_barrier_semaphore()
    hub = p == HUB
    for k in range(1, LINE):
        q = lax.rem(p + k, LINE)

        @pl.when(q != HUB)
        def _():
            pl.semaphore_signal(barrier, inc=1, device_id=in_line(q), device_id_type=MESH)

    def remote(src, dst, s_sem, r_sem, peer):
        return pltpu.make_async_remote_copy(
            src_ref=src, dst_ref=dst, send_sem=s_sem, recv_sem=r_sem, device_id=peer,
            device_id_type=MESH,
        )

    tmp[...] = jnp.zeros_like(tmp)
    inputs[0].wait()
    tmp[pl.ds(pl.multiple_of(sx * 32, 32), 32), :] = react[...]
    rsend[...] = tmp[...].T
    inputs[1].wait()
    inputs[2].wait()
    opening = jnp.where(ta == 0, 1.0 / STEP, 0.0)
    for m in range(8):
        b = m % 4
        q = lax.rem(m // 4 + ta, 2)
        planes = [f[8 * b + 2 * g + q] for g in range(4)]
        if m == 0:
            planes[0] = planes[0] + opening * init[...]
        S[pl.ds(m, 128, stride=8), :] = jnp.concatenate(planes, axis=0).T

    @pl.when(jnp.logical_not(hub))
    def _():
        pl.semaphore_wait(barrier, LINE - 1)

    @pl.when(p == HUB - 1)
    def _():
        pl.semaphore_signal(near, inc=1, device_id=in_line(HUB), device_id_type=MESH)

    @pl.when(hub)
    def _():
        pl.semaphore_wait(near, 1)

        def greet(k, carry):
            pl.semaphore_signal(barrier, inc=1, device_id=in_plane(k), device_id_type=MESH)
            return carry

        lax.fori_loop(1, nsy, greet, 0)


    copies_c = []
    for k in range(1, 4):
        to = lax.rem(sx + k, 4)
        q = 4 * (to // 2) + 2 * ta + to % 2
        rows = pl.ds(pl.multiple_of(slice_of(q) * OWN, OWN), OWN)
        c = remote(rsend.at[rows], rrecv.at[sx], c_s.at[k], c_r.at[k],
                   {"sx": to, "sy": sy, "ta": ta})
        c.start()
        copies_c.append(c)
    copies_a = [[], []]
    for h in range(2):
        slots = pl.ds(64 * h, 64)

        def rows_of(q):
            return pl.ds(pl.multiple_of(slice_of(q) * 128 + 64 * h, 64), 64)

        for k in range(1, LINE):
            q = lax.rem(p + k, LINE)
            copies_a[h].append(remote(S.at[rows_of(q)], rcv.at[p, slots], a_s.at[8 * h + k],
                                      a_r.at[8 * h + k], in_line(q)))
        copies_a[h].append(
            pltpu.make_async_copy(S.at[rows_of(p)], rcv.at[p, slots], l_s.at[h]))
        for c in copies_a[h]:
            c.start()
    rrecv[sx] = rsend[pl.ds(pl.multiple_of(d * OWN, OWN), OWN), :]
    for c in copies_c:
        c.wait()
    rext[pl.ds(HALO, OWN), :] = (rrecv[0] + rrecv[1]) + (rrecv[2] + rrecv[3])

    def edges(src, left_dst, right_dst, k):
        return (
            remote(src.at[pl.ds(HALO, HALO)], left_dst, h_s.at[2 * k], h_r.at[2 * k], left),
            remote(src.at[pl.ds(OWN, HALO)], right_dst, h_s.at[2 * k + 1], h_r.at[2 * k + 1],
                   right),
        )

    def halos(ref, k):
        return edges(ref, ref.at[pl.ds(ENDS, HALO)], ref.at[pl.ds(0, HALO)], k)

    halo_c = halos(rext, 0)

    sub = iota(0)
    lane = iota(1)
    first = sub == 0

    def coefficients(cols, inside):
        for col in cols:
            r = jnp.broadcast_to(rext[pl.ds(col, 1), :], (8, 128))
            c = 1.0 / (1.0 / STEP + 4.0 + r)
            cp = c / STEP
            up = (1.0 / STEP + 4.0 + r) * STEP
            q2 = cp * cp
            q4 = q2 * q2
            q = q4 * q4
            qq = q * q
            qqqq = qq * qq
            cl = c * inside
            pw = inside
            for l in range(8):
                CL[col, part(l), :] = cl
                cl = cl * up
                if l:
                    pw = pw * cp
                    PW[col, part(l), :] = pw
            KS[col, part(0), :] = jnp.where(sub < 1, ALPHA * q, q)
            KS[col, part(1), :] = jnp.where(sub < 2, ALPHA * qq, qq)
            KS[col, part(2), :] = jnp.where(sub < 4, ALPHA * qqqq, qqqq)
            ks = inside * cp / (1.0 - ALPHA * (qqqq * qqqq))
            KS[col, part(3), :] = jnp.where(first, ALPHA * ks, ks)

    def solve(g, col):
        v = [g[0]]
        for l in range(1, 8):
            v.append(v[-1] + g[l])
        a = PW[col, part(7), :] * v[7]
        a = a + KS[col, part(0), :] * pltpu.roll(a, 1, 0)
        a = a + KS[col, part(1), :] * pltpu.roll(a, 2, 0)
        a = a + KS[col, part(2), :] * pltpu.roll(a, 4, 0)
        s = KS[col, part(3), :] * pltpu.roll(a, 1, 0)
        return [v[0] + s] + [PW[col, part(l), :] * (v[l] + s) for l in range(1, 8)]

    def rows_beside(v):
        return (jnp.where(lane == 0, 0.0, pltpu.roll(v, 1, 1))
                + jnp.where(lane == 127, 0.0, pltpu.roll(v, 127, 1)))

    def first_sweep(cols):
        done = []
        for col in cols:
            g = []
            for l in range(8):
                g.append(CL[col, part(l), :] * Rx[col, part(l), :])
            done.append((col, g, solve(g, col)))
        for col, g, u in done:
            for l in range(8):
                CR[col, part(l), :] = g[l]
                U0[col, part(l), :] = u[l]

    def around(U, col):
        return [
            (U[col - 1, part(l), :] + U[col + 1, part(l), :]) + rows_beside(U[col, part(l), :])
            for l in range(8)
        ]

    def at_corner(U, col):
        return jnp.where(first, CORNER * pltpu.roll(U[col, part(7), :], 1, 0), 0.0)

    def sweep(src, dst, cols, keep=False):
        done = []
        for col in cols:
            n = around(src, col)
            g = [CR[col, part(l), :] + CL[col, part(l), :] * n[l] for l in range(8)]
            done.append((col, n, solve(g, col)))
        for col, n, u in done:
            for l in range(8):
                dst[col, part(l), :] = u[l]
                if keep:
                    NB[col, part(l), :] = n[l]

    def turning_sweep(src, dst, cols, acc):
        done = []
        for col in cols:
            n = around(src, col)
            e = at_corner(src, col)
            c0 = CR[col, part(0), :] - CL[col, part(0), :] * e
            g = [c0 + CL[col, part(0), :] * n[0]]
            g += [CR[col, part(l), :] + CL[col, part(l), :] * n[l] for l in range(1, 8)]
            for l in range(8):
                r = n[l] - NB[col, part(l), :]
                if l == 0:
                    r = r - e
                acc = acc + r * r
            done.append((col, e, c0, solve(g, col)))
        for col, e, c0, u in done:
            E[col] = e
            CR[col, part(0), :] = c0
            for l in range(8):
                dst[col, part(l), :] = u[l]
        return acc

    def spread(lo, count, fn, carry=0, each=UNROLL):
        def step(i, carry):
            base = lo + each * i
            out = fn([base + k for k in range(each)], carry)
            return carry if out is None else out

        return lax.fori_loop(0, count // each, step, carry)

    spread(HALO, OWN, lambda cols, _: coefficients(cols, 1.0), each=1)

    @pl.when(hub)
    def _():
        pl.semaphore_wait(barrier, nsy - 1)
        for q in range(LINE - 1):
            pl.semaphore_signal(far, inc=1, device_id=in_line(q), device_id_type=MESH)


    def unpack(cols, acc):
        for col in cols:
            rows = pl.ds(pl.multiple_of(8 * col, 8), 8)
            w = []
            for t in range(2):
                v = [rcv[4 * (s // 2) + 2 * t + s % 2, rows, :] for s in range(4)]
                w.append(swap_groups(v))
            for g in range(4):
                even = jnp.where(sub < 4, w[0][g], w[1][g])
                other = pltpu.roll(jnp.where(sub < 4, w[1][g], w[0][g]), 4, 0)
                Rx[HALO + col, part(2 * g), :] = even
                Rx[HALO + col, part(2 * g + 1), :] = other
                acc = acc + even * even + other * other
        return acc

    nothing = jnp.zeros((8, 128), jnp.float32)
    halo_r = halos(Rx, 1)
    acc0 = nothing
    for h in range(2):
        for c in copies_a[h]:
            c.wait()
        acc0 = spread(HALO * h, HALO, unpack, acc0, each=2)
        if h == 0:
            @pl.when(jnp.logical_not(hub))
            def _():
                pl.semaphore_wait(far, 1)

            for c in halo_c:
                c.start()
        halo_r[h].start()
    spread(HALO, OWN, lambda cols, _: first_sweep(cols), each=2)

    def inner(j0, k, src, dst, keep=False):
        sweep(src, dst, [HALO + k + i for i in range(OWN - 2 * k)], keep)

    for i in range(3):
        inner(0, 2 * i + 1, U0, U1)
        inner(0, 2 * i + 2, U1, U0)
    inner(0, 7, U0, U1, True)

    at_start = jnp.logical_and(sy == 0, d == 0)
    at_end = jnp.logical_and(sy == nsy - 1, d == 7)
    in_left = jnp.where(at_start, 0.0, 1.0)
    in_right = jnp.where(at_end, 0.0, 1.0)

    def strip(lo, way, src, dst, k, keep=False):
        spread(lo + way * k, HALO, lambda cols, _: sweep(src, dst, cols, keep))

    def strip_a(lo, way, acc):
        spread(0 if way > 0 else ENDS, HALO, lambda cols, _: first_sweep(cols), each=2)

        def pair(i, carry):
            strip(lo, way, U0, U1, 2 * i + 1)
            strip(lo, way, U1, U0, 2 * i + 2)
            return carry

        lax.fori_loop(0, 3, pair, 0)
        strip(lo, way, U0, U1, 7, True)
        return spread(lo + way * 8, HALO, lambda cols, a: turning_sweep(U1, V0, cols, a), acc)

    to_left, to_right = halos(V0, 2)
    e_left, e_right = halos(E, 3)
    halo_c[0].wait()
    spread(ENDS, HALO, lambda cols, _: coefficients(cols, in_right), each=1)
    halo_r[0].wait()
    acc1 = strip_a(ENDS, -1, nothing)
    to_right.start()
    e_right.start()
    halo_c[1].wait()
    spread(0, HALO, lambda cols, _: coefficients(cols, in_left), each=1)
    halo_r[1].wait()
    acc1 = strip_a(0, 1, acc1)
    to_left.start()
    e_left.start()

    inner(9, 1, V0, U1)

    for i in range(2):
        inner(9, 2 * i + 2, U1, U0)
        inner(9, 2 * i + 3, U0, U1)
    inner(9, 6, U1, U0)
    inner(9, 7, U0, U1, True)

    def change_rhs(cols, _):
        for col in cols:
            CR[col, part(0), :] = CR[col, part(0), :] - CL[col, part(0), :] * E[col]

    def strip_b(lo, way, outside):
        @pl.when(outside)
        def _():
            def clear(cols, _):
                for col in cols:
                    V0[col] = jnp.zeros((64, 128), jnp.float32)

            spread(0 if way > 0 else ENDS, HALO, clear, each=1)

        spread(0 if way > 0 else ENDS, HALO, change_rhs)
        strip(lo, way, V0, U1, 1)

        def pair(i, carry):
            strip(lo, way, U1, U0, 2 * i + 2)
            strip(lo, way, U0, U1, 2 * i + 3)
            return carry

        lax.fori_loop(0, 2, pair, 0)
        strip(lo, way, U1, U0, 6)
        strip(lo, way, U0, U1, 7, True)

    def left_over(cols, acc):
        for col in cols:
            n = around(U1, col)
            for l in range(8):
                r = n[l] - NB[col, part(l), :]
                if l == 0:
                    r = r + (E[col] - at_corner(U1, col))
                acc = acc + r * r
        return acc


    def pack(cols, _):
        for col in cols:
            rows = pl.ds(pl.multiple_of(8 * col, 8), 8)
            w = [[], []]
            for g in range(4):
                even = U1[HALO + col, part(2 * g), :]
                other = pltpu.roll(U1[HALO + col, part(2 * g + 1), :], 4, 0)
                w[0].append(jnp.where(sub < 4, even, other))
                w[1].append(jnp.where(sub < 4, other, even))
            for t in range(2):
                v = swap_groups(w[t])
                for s in range(4):
                    M[4 * (s // 2) + 2 * t + s % 2, rows, :] = v[s]

    copies_o = []

    def send_out(h):
        slot = pl.ds(pl.multiple_of(d * 128 + 64 * h, 64), 64)
        rows = pl.ds(64 * h, 64)
        for k in range(1, LINE):
            q = lax.rem(p + k, LINE)
            copies_o.append(remote(M.at[q, rows], O.at[slot], o_s.at[8 * h + k],
                                   o_r.at[8 * h + k], in_line(q)))
            copies_o[-1].start()
        copies_o.append(pltpu.make_async_copy(M.at[p, rows], O.at[slot], l_s.at[2 + h]))
        copies_o[-1].start()

    to_right.wait()
    e_right.wait()
    strip_b(0, 1, at_start)
    acc2 = spread(HALO, OWN // 2, left_over, nothing, each=4)
    spread(0, OWN // 2, pack, each=2)
    send_out(0)
    to_left.wait()
    e_left.wait()
    strip_b(ENDS, -1, at_end)
    acc2 = spread(HALO + OWN // 2, OWN // 2, left_over, acc2, each=4)

    def total(v):
        return jnp.sum(v, axis=0, keepdims=True)

    redx[p] = jnp.where(sub == 0, total(acc0), jnp.where(sub == 1, total(acc1), jnp.where(
        sub == 2, total(acc2), 0.0)))
    copies_x = []
    for k in range(1, LINE):
        c = remote(redx.at[p], redx.at[p], x_s.at[k], x_r.at[k], in_line(lax.rem(p + k, LINE)))
        c.start()
        copies_x.append(c)

    spread(OWN // 2, OWN // 2, pack, each=2)
    send_out(1)
    for c in copies_x:
        c.wait()
    sums = redx[0]
    for k in range(1, LINE):
        sums = sums + redx[k]
    redz[sy] = sums

    def plane(k):
        return remote(redz.at[sy], redz.at[sy], z_s.at[k], z_r.at[k], in_plane(k))

    def send(k, carry):
        plane(k).start()
        return carry

    lax.fori_loop(1, nsy, send, 0)

    for c in copies_o:
        c.wait()
    def arrive(k, carry):
        plane(k).wait()
        return carry

    lax.fori_loop(1, nsy, arrive, 0)
    sums = redz[0]
    for k in range(1, nsy):
        sums = sums + redz[k]
    stat[...] = sums


def turn(cells, turned, sums, out, stat, done, o_s):
    ta = lax.axis_index("ta")
    copies = []
    for m in range(8):
        b = m % 4
        q = lax.rem(m // 4 + ta, 2)
        x = turned[pl.ds(m, 128, stride=8), :].T
        for g in range(4):
            done[m, g] = x[32 * g:32 * g + 32, :]
            copies.append(pltpu.make_async_copy(
                done.at[m, g], out.at[8 * b + 2 * g + q], o_s.at[4 * m + g]))
            copies[-1].start()
    for i in range(3):
        stat[i] = jnp.sum(sums[i:i + 1, :]) / cells
    for c in copies:
        c.wait()


def solution(mesh):
    nsy = mesh.shape["sy"]
    ny, nz = (4, 8) if nsy == 32 else (2, nsy // 2)

    def step(forcing, react, initial):
        vmem = pl.BlockSpec(memory_space=pltpu.VMEM)
        dma = pltpu.SemaphoreType.DMA
        f32 = jnp.float32
        turned, sums = pl.pallas_call(
            functools.partial(kernel, ny, nz),
            out_shape=(
                jax.ShapeDtypeStruct((1024, 128), f32),
                jax.ShapeDtypeStruct((8, 128), f32),
            ),
            in_specs=[pl.BlockSpec(memory_space=pltpu.HBM)] * 3,
            out_specs=(pl.BlockSpec(memory_space=pltpu.HBM), vmem),
            scratch_shapes=[
                pltpu.VMEM((32, 32, 128), f32),
                pltpu.VMEM((32, 128), f32),
                pltpu.VMEM((32, 128), f32),
                pltpu.VMEM((1024, 128), f32),
                pltpu.VMEM((8, 128, 128), f32),
                pltpu.VMEM((128, 128), f32),
                pltpu.VMEM((128, 128), f32),
                pltpu.VMEM((4, OWN, 128), f32),
                pltpu.VMEM((WIDE, 128), f32),
            ] + [pltpu.VMEM((WIDE, 64, 128), f32)] * 8 + [
                pltpu.VMEM((WIDE, 32, 128), f32),
                pltpu.VMEM((WIDE, 8, 128), f32),
                pltpu.VMEM((8, 128, 128), f32),
                pltpu.VMEM((LINE, 8, 128), f32),
                pltpu.VMEM((ny * nz, 8, 128), f32),
                dma((16,)), dma((16,)), dma((4,)), dma((4,)), dma((8,)), dma((8,)),
                dma((16,)), dma((16,)), dma((8,)), dma((8,)),
                dma((ny * nz,)), dma((ny * nz,)), dma((7,)),
                pltpu.SemaphoreType.REGULAR, pltpu.SemaphoreType.REGULAR,
            ],
            compiler_params=pltpu.CompilerParams(
                collective_id=0, has_side_effects=True, vmem_limit_bytes=67043328
            ),
        )(forcing, react, initial)
        return pl.pallas_call(
            functools.partial(turn, 64.0 * 128.0 * 128.0 * nsy),
            out_shape=(
                jax.ShapeDtypeStruct((32, 32, 128), f32),
                jax.ShapeDtypeStruct((3,), f32),
            ),
            in_specs=[vmem] * 2,
            out_specs=(pl.BlockSpec(memory_space=pltpu.HBM), pl.BlockSpec(memory_space=pltpu.SMEM)),
            scratch_shapes=[pltpu.VMEM((8, 4, 32, 128), f32), dma((32,))],
            compiler_params=pltpu.CompilerParams(vmem_limit_bytes=TURN_VMEM),
        )(turned, sums)

    placed = (P("ta", "sx", "sy"), P("sx", "sy"), P("sx", "sy"))
    return jax.shard_map(
        step, mesh=mesh, in_specs=placed, out_specs=(P("ta", "sx", "sy"), P(None)),
        check_vma=False,
    )
```
